128 devices in a mesh: tile: 64 (over z, x, y_lo, core), chan: 2 (over y_hi).
Axes of the slice: x: 4, y: 4 (y_hi: 2, y_lo: 2; y = y_hi * 2 + y_lo), z: 4, core: 2. Of those that a mesh axis runs over, the one named last changes fastest.
Arguments:
- inputs: bfloat16 [128, 64, 4096], P('tile', 'chan'), may hold values from -6 to 6
- gluing: int32 [128, 4, 3], P('tile'), may hold values from 0 to 127, as said below
- conv_weight: bfloat16 [64, 64, 3, 3], replicated, may hold values from -0.25 to 0.25
- level_weight: bfloat16 [128, 64, 2, 2], replicated, may hold values from -0.375 to 0.375
- cotangent: bfloat16 [128, 128, 1024], P('tile', 'chan'), may hold values from -6 to 6
Outputs:
- level: bfloat16 [128, 128, 1024], P('tile', 'chan')
- grad_inputs: bfloat16 [128, 64, 4096], P('tile', 'chan')
- grad_conv: float32 [64, 64, 3, 3], P(None, 'chan')
- grad_level: float32 [128, 64, 2, 2], P(None, 'chan')
The draws below stay inside these ranges and needn't reach their ends.
Inputs may be any that keep to these rules, and one draw needn't show every extreme that they name: Entry [t, s] = (u, r, f) with r in 0..3 and f in 0..1 says that side s of tile t is glued to side r of tile u; the gluing is symmetric: entry [u, r] is (t, s, f), and no side is glued to itself.
All inputs are finite; a program needn't handle non-finite values.
Results may differ from the reference program's by a relative error of at most 0.005.
Values may be sent and summed in bfloat16 or wider, within the bound.
No kernel may reach another device: no remote copies, remote signals or barrier semaphores. Data moves between devices by JAX's collectives and lax.ppermute only.
A program may use at most 128 MiB of HBM per device.

```python
import jax
import jax.numpy as jnp
from jax import lax

C = 64
CO = 128
S = 64
TILES = 128


def draw_gluing(key, part):
    edge_count = 4 * TILES
    order = jax.random.permutation(key, edge_count).astype(jnp.int32)
    first = order[0::2]
    second = order[1::2]
    flips = jax.random.randint(jax.random.fold_in(key, 7), (edge_count // 2,), 0, 2).astype(jnp.int32)
    partner = jnp.zeros((edge_count,), jnp.int32).at[first].set(second).at[second].set(first)
    flipped = jnp.zeros((edge_count,), jnp.int32).at[first].set(flips).at[second].set(flips)
    stacked = jnp.stack([partner // 4, partner % 4, flipped], axis=-1)
    return stacked.reshape(TILES, 4, 3).astype(jnp.int32)


def levels(stream_key, shape, cuts, low, high):
    loudness, own = 1.0, jax.random.fold_in(stream_key, 6)
    for position, parts in cuts:
        heights = jnp.exp(jax.random.uniform(jax.random.fold_in(own, position), (parts,), jnp.float32, low / len(cuts), high / len(cuts)))
        loudness = loudness * jnp.repeat(heights, shape[position] // parts).reshape([-1 if axis == position else 1 for axis in range(len(shape))])
    return loudness


def gaussian(rng, shape, scale, bound, shards=(), kind=jnp.bfloat16):
    drawn = scale * jax.random.normal(rng, shape, jnp.float32)
    if shards:
        drawn = drawn * levels(rng, shape, shards, -0.22, 0.18)
    return jnp.clip(drawn, -bound, bound).astype(kind)


def setup_inputs(seed: int = 0) -> dict:
    key_list = jax.random.split(jax.random.key(seed), 6)
    inputs = gaussian(key_list[0], (TILES, C, S * S), 1.0, 6.0, ((0, 64), (1, 2)))
    gluing = draw_gluing(jax.random.fold_in(key_list[5], 71), 0)
    conv_weight = gaussian(key_list[2], (C, C, 3, 3), (9 * C) ** -0.5, 0.25)
    level_weight = gaussian(key_list[3], (CO, C, 2, 2), (4 * C) ** -0.5, 0.375)
    cotangent = gaussian(key_list[4], (TILES, CO, (S // 2) * (S // 2)), 1.0, 6.0, ((0, 64), (1, 2)))
    return {"inputs": inputs, "gluing": gluing, "conv_weight": conv_weight, "level_weight": level_weight, "cotangent": cotangent}


def edge_strips(source):
    return jnp.stack([source[:, :, 0, :], source[:, :, -1, :], source[:, :, :, 0], source[:, :, :, -1]], axis=1)

def border_strips(padded):
    return jnp.stack([padded[:, :, 0, 1:-1], padded[:, :, -1, 1:-1], padded[:, :, 1:-1, 0], padded[:, :, 1:-1, -1]], axis=1)

def orient(strips, gluing):
    return jnp.where(gluing[:, :, 2][:, :, None, None] == 1, strips[..., ::-1], strips)

def assemble(source, halo_cells):
    tile_count, chan_count = (source.shape[0], source.shape[1])
    corner = jnp.zeros((tile_count, chan_count, 1), source.dtype)
    top_row = jnp.concatenate([corner, halo_cells[:, 0], corner], axis=2)[:, :, None, :]
    low_row = jnp.concatenate([corner, halo_cells[:, 1], corner], axis=2)[:, :, None, :]
    middle = jnp.concatenate([halo_cells[:, 2][:, :, :, None], source, halo_cells[:, 3][:, :, :, None]], axis=3)
    return jnp.concatenate([top_row, middle, low_row], axis=2)

def conv_three(padded, weight):
    extent = padded.shape[2] - 2
    summed = None
    for row_tap in range(3):
        for col_tap in range(3):
            product_term = jnp.einsum('oc,ncxy->noxy', weight[:, :, row_tap, col_tap], padded[:, :, row_tap:row_tap + extent, col_tap:col_tap + extent], preferred_element_type=jnp.float32)
            summed = product_term if summed is None else summed + product_term
    return summed

def conv_two(hidden, weight):
    tile_count, chan_count, extent = (hidden.shape[0], hidden.shape[1], hidden.shape[2])
    summed = None
    for row_tap in range(2):
        for col_tap in range(2):
            sampled = hidden[:, :, row_tap::2, col_tap::2].reshape(tile_count, chan_count, -1)
            product_term = jnp.einsum('oc,ncp->nop', weight[:, :, row_tap, col_tap], sampled, preferred_element_type=jnp.float32)
            summed = product_term if summed is None else summed + product_term
    return summed.reshape(tile_count, weight.shape[0], extent // 2, extent // 2)

def level_grads(hidden, cot_full, weight):
    tile_count, chan_count, extent = (hidden.shape[0], hidden.shape[1], hidden.shape[2])
    half = extent // 2
    cot_rows = cot_full.reshape(tile_count, cot_full.shape[1], -1)
    weight_rows = []
    spread_rows = []
    for row_tap in range(2):
        weight_cols = []
        spread_cols = []
        for col_tap in range(2):
            sampled = hidden[:, :, row_tap::2, col_tap::2].reshape(tile_count, chan_count, -1)
            weight_cols.append(jnp.einsum('nop,ncp->oc', cot_rows, sampled, preferred_element_type=jnp.float32))
            spread = jnp.einsum('oc,nop->ncp', weight[:, :, row_tap, col_tap], cot_rows, preferred_element_type=jnp.float32)
            spread_cols.append(spread.reshape(tile_count, chan_count, half, half))
        weight_rows.append(jnp.stack(weight_cols, axis=-1))
        spread_rows.append(jnp.stack(spread_cols, axis=-1))
    grad_weight = jnp.stack(weight_rows, axis=2)
    grad_hidden = jnp.stack(spread_rows, axis=3).reshape(tile_count, chan_count, extent, extent)
    return (grad_weight, grad_hidden)

def conv_grads(padded, grad_full, weight):
    extent = padded.shape[2] - 2
    grad_padded = jnp.zeros(padded.shape, jnp.float32)
    weight_rows = []
    for row_tap in range(3):
        weight_cols = []
        for col_tap in range(3):
            window = padded[:, :, row_tap:row_tap + extent, col_tap:col_tap + extent]
            weight_cols.append(jnp.einsum('noxy,ncxy->oc', grad_full, window, preferred_element_type=jnp.float32))
            spread = jnp.einsum('oc,noxy->ncxy', weight[:, :, row_tap, col_tap], grad_full, preferred_element_type=jnp.float32)
            grad_padded = grad_padded.at[:, :, row_tap:row_tap + extent, col_tap:col_tap + extent].add(spread)
        weight_rows.append(jnp.stack(weight_cols, axis=-1))
    return (jnp.stack(weight_rows, axis=2), grad_padded)

def reference(inputs, gluing, conv_weight, level_weight, cotangent):
    tile_count = inputs.shape[0]
    inputs = inputs.reshape(tile_count, inputs.shape[1], S, S)
    cotangent = cotangent.reshape(tile_count, cotangent.shape[1], S // 2, S // 2)
    target = (gluing[:, :, 0] * 4 + gluing[:, :, 1]).reshape(-1).astype(jnp.int32)

    def route(strips):
        rows_flat = strips.reshape((tile_count * 4,) + strips.shape[2:])
        chosen = jnp.take(rows_flat, target, axis=0).reshape(strips.shape)
        return orient(chosen, gluing)
    padded = assemble(inputs, route(edge_strips(inputs)))
    conv_float = conv_weight.astype(jnp.float32)
    level_float = level_weight.astype(jnp.float32)

    def per_tile(pair):
        padded_tile = pair[0][None].astype(jnp.float32)
        cot_tile = pair[1][None].astype(jnp.float32)
        pre_act = conv_three(padded_tile, conv_float)
        hidden = jax.nn.gelu(pre_act).astype(jnp.bfloat16)
        level = conv_two(hidden.astype(jnp.float32), level_float).astype(jnp.bfloat16)
        grad_level, grad_hidden = level_grads(hidden.astype(jnp.float32), cot_tile, level_float)
        unused, pullback = jax.vjp(jax.nn.gelu, pre_act)
        grad_pre = pullback(grad_hidden)[0].astype(jnp.bfloat16)
        grad_conv, grad_padded = conv_grads(padded_tile, grad_pre.astype(jnp.float32), conv_float)
        rims = border_strips(grad_padded).astype(jnp.bfloat16)
        return (level[0], grad_conv, grad_level, rims[0], grad_padded[0, :, 1:-1, 1:-1])
    level, conv_terms, level_terms, rims, interior = lax.map(per_tile, (padded, cotangent))
    returned = route(rims).astype(jnp.float32)
    interior = interior.at[:, :, 0, :].add(returned[:, 0])
    interior = interior.at[:, :, -1, :].add(returned[:, 1])
    interior = interior.at[:, :, :, 0].add(returned[:, 2])
    interior = interior.at[:, :, :, -1].add(returned[:, 3])
    grad_conv = lax.optimization_barrier(jnp.sum(conv_terms, axis=0))
    grad_level = lax.optimization_barrier(jnp.sum(level_terms, axis=0))
    level = level.reshape(tile_count, level.shape[1], -1)
    grad_inputs = interior.astype(jnp.bfloat16).reshape(tile_count, interior.shape[1], -1)
    return (level, grad_inputs, grad_conv, grad_level)
```

```python
import functools

import jax
import jax.numpy as jnp
import numpy as np
from jax import lax
from jax.experimental import pallas as pl
from jax.experimental.pallas import tpu as pltpu
from jax.sharding import Mesh
from jax.sharding import PartitionSpec as P

BF = jnp.bfloat16
F32 = jnp.float32
NT = (((1,), (1,)), ((), ()))
SQ = float(np.sqrt(2.0 / np.pi))


def constants():
    perm = np.zeros((512, 512), np.float32)
    for i in range(8):
        for j in range(64):
            perm[i * 64 + j, ((i % 2) * 2 + j % 2) * 128 + (i // 2) * 32 + j // 2] = 1
    edge = np.zeros((128, 2048), np.float32)
    for side in range(2):
        for a in range(2):
            for x in range(32):
                edge[side * 64 + a * 32 + x, a * 1024 + x * 32 + 31 * side] = 1
    rev = np.zeros((128, 128), np.float32)
    for half in range(2):
        for i in range(64):
            rev[half * 64 + i, half * 64 + 63 - i] = 1
    spread = np.zeros((256, 4096), np.float32)
    for b in range(2):
        for y in range(32):
            k = b * 32 + y
            spread[k, 2 * y + b] = 1
            spread[64 + k, 63 * 64 + 2 * y + b] = 1
            spread[128 + k, (2 * y + b) * 64] = 1
            spread[192 + k, (2 * y + b) * 64 + 63] = 1
    return [jnp.asarray(m, BF) for m in (perm, edge, rev, spread)]


def dot(a, b):
    return jnp.dot(a, b, preferred_element_type=F32)


def dot_nt(a, b):
    return lax.dot_general(a, b, NT, preferred_element_type=F32)


def al(v, m):
    return pl.multiple_of(v, m)


def split(v):
    hi = v.astype(BF)
    return hi, (v - hi.astype(F32)).astype(BF)


def strips_kernel(meta, inp, spread, out):
    both = inp[...].reshape(64, 4096)
    s = dot_nt(both, spread[...]).astype(BF)
    for tile in range(2):
        for pair in range(2):
            row = (tile * 2 + pair) * 32
            out[row : row + 32, :] = s[tile * 32 : tile * 32 + 32, pair * 128 : pair * 128 + 128]
    lane = lax.broadcasted_iota(jnp.int32, (16, 128), 1)
    codes = jnp.zeros((16, 128), jnp.int32)
    for k in range(24):
        codes = jnp.where(lane == k, meta[k], codes)
    out[128:144, :] = codes.astype(F32).astype(BF)


def send_kernel(meta, inp, cot, out_in, out_cot):
    o = 1 - meta[24]
    out_in[...] = inp[o]
    out_cot[...] = cot[o]


def weight_kernel(w, wt, wb, wbt):
    wb[...] = jnp.zeros((256, 1024), BF)
    wbt[...] = jnp.zeros((1024, 256), BF)
    for a in range(2):
        for b in range(2):
            ab = (a * 2 + b) * 64
            for i in range(3):
                for j in range(3):
                    rs = ((a + i) * 4 + b + j) * 64
                    wb[ab : ab + 64, rs : rs + 64] = w[i, j]
                    wbt[rs : rs + 64, ab : ab + 64] = wt[i, j]


def place(acc, row, v, src_side, dst_side, half):
    v = pltpu.roll(v, ((src_side ^ dst_side) & 1) * 64, 1)
    acc[pl.ds(row, 32), :] = jnp.where(half == (dst_side & 1), v, acc[pl.ds(row, 32), :])


def route_strips_kernel(meta, codes, b0, b1, b2, b3, *rest):
    outs, acc = rest[:8], rest[8]
    acc[...] = jnp.zeros((512, 128), F32)
    half = lax.broadcasted_iota(jnp.int32, (32, 128), 1) // 64
    lch, zx = meta[25], meta[27]
    for bi, bundle in enumerate((b0, b1, b2, b3)):

        @pl.loop(0, 32)
        def _(m, bi=bi, bundle=bundle):
            base = (bi * 32 + m) * 3
            t = codes[base]
            s = codes[base + 1]
            r = m & 3

            @pl.when((t >> 3) == zx)
            def _():
                k = (t & 7) ^ lch
                row = al((m >> 3) * 144 + ((m >> 2) & 1) * 64 + (r >> 1) * 32, 16)
                v = bundle[pl.ds(row, 32), :].astype(F32)
                place(acc, al(k * 64 + (s >> 1) * 32, 32), v, r, s, half)

    for k in range(8):
        outs[k][...] = acc[k * 64 : k * 64 + 64, :].astype(BF)


def flip(strips, rev, first, second):
    n = strips.shape[0]
    turned = dot(strips.astype(BF), rev)
    lane = lax.broadcasted_iota(jnp.int32, (n, 128), 1)
    flag = jnp.where(lane < 64, first, second)
    return jnp.where(flag == 1, turned, strips)


def main_kernel(
    meta, inp, rin, cot, rcot, h0, h1, h2, h3, h4, h5, h6, h7, wb, wbt, lw, lwt, perm, edge, rev,
    gxk, gxs, lvk, lvs, rim, wown, p1, p2, p3,
    xs, pt, ct, tb_s, lr_s, pre_s, gh_s, hd, gp, wh, lv_s,
):
    h, xi = meta[24], meta[26]
    mine, other = h * 32, 32 - h * 32
    for g in range(8):
        xs[pl.ds(al(g * 64 + mine, 32), 32), :] = inp[h, :, g * 512 : g * 512 + 512]
        xs[pl.ds(al(g * 64 + other, 32), 32), :] = rin[:, g * 512 : g * 512 + 512]
    ct[pl.ds(al(h * 64, 64), 64), :] = cot[h]
    ct[pl.ds(al(64 - h * 64, 64), 64), :] = rcot[...]
    nat = dot(xs[...], perm[...])
    ph = [
        [
            jnp.concatenate(
                [nat[g * 64 : g * 64 + 64, (a * 2 + b) * 128 : (a * 2 + b) * 128 + 128] for g in range(8)],
                axis=1,
            )
            for b in range(2)
        ]
        for a in range(2)
    ]
    own = (h0[...].astype(F32) + h2[...].astype(F32)) + (h4[...].astype(F32) + h6[...].astype(F32))
    far = (h1[...].astype(F32) + h3[...].astype(F32)) + (h5[...].astype(F32) + h7[...].astype(F32))
    for ref, k in ((tb_s, 0), (lr_s, 32)):
        ref[pl.ds(al(mine, 32), 32), :] = own[k : k + 32]
        ref[pl.ds(al(other, 32), 32), :] = far[k : k + 32]
    fl = [meta[(h * 4 + s) * 3 + 2] for s in range(4)]
    tb = flip(tb_s[...], rev[...], fl[0], fl[1])
    lr = flip(lr_s[...], rev[...], fl[2], fl[3])
    sp = dot(lr.astype(BF), edge[...])
    lane = lax.broadcasted_iota(jnp.int32, (64, 1024), 1)
    y = lane & 31
    l1 = lax.broadcasted_iota(jnp.int32, (64, 128), 1)
    cols = [[None] * 4 for _ in range(2)]
    for a in range(2):
        spa = sp[:, a * 1024 : a * 1024 + 1024]
        cols[a][0] = jnp.where(y == 0, spa, pltpu.roll(ph[a][1], 1, 1))
        cols[a][1] = ph[a][0]
        cols[a][2] = ph[a][1]
        cols[a][3] = jnp.where(y == 31, spa, pltpu.roll(ph[a][0], 1023, 1))
    top_shift = (97, 0, 96, 127)
    low_shift = (1, 32, 0, 31)
    for s in range(4):
        pt[(4 + s) * 64 : (4 + s) * 64 + 64, :] = cols[0][s].astype(BF)
        pt[(8 + s) * 64 : (8 + s) * 64 + 64, :] = cols[1][s].astype(BF)
        up = pltpu.roll(cols[1][s], 32, 1)
        t = pltpu.roll(tb, top_shift[s], 1) if top_shift[s] else tb
        if s == 0:
            t = jnp.where(l1 == 0, 0.0, t)
        if s == 3:
            t = jnp.where(l1 == 31, 0.0, t)
        pt[s * 64 : s * 64 + 64, 128:] = up[:, 128:].astype(BF)
        pt[s * 64 : s * 64 + 64, :128] = jnp.where(l1 < 32, t, up[:, :128]).astype(BF)
        dn = pltpu.roll(cols[0][s], 992, 1)
        t = pltpu.roll(tb, low_shift[s], 1) if low_shift[s] else tb
        if s == 0:
            t = jnp.where(l1 == 96, 0.0, t)
        if s == 3:
            t = jnp.where(l1 == 127, 0.0, t)
        pt[(12 + s) * 64 : (12 + s) * 64 + 64, :896] = dn[:, :896].astype(BF)
        pt[(12 + s) * 64 : (12 + s) * 64 + 64, 896:] = jnp.where(l1 >= 96, t, dn[:, 896:]).astype(BF)
    pre_s[...] = dot(wb[...], pt[...])
    gh_s[...] = dot(lwt[...], ct[...])
    for q in range(8):
        rows = slice(q * 32, q * 32 + 32)
        v = pre_s[rows, :]
        v2 = v * v
        th = jnp.tanh(SQ * (v + 0.044715 * (v2 * v)))
        half = 0.5 * (1.0 + th)
        hd[rows, :] = (v * half).astype(BF)
        d = half + 0.5 * v * (1.0 - th * th) * (SQ * (1.0 + 3 * 0.044715 * v2))
        gp[rows, :] = (gh_s[rows, :] * d).astype(BF)
    gx = dot(wbt[...], gp[...])

    def blk(r, s):
        k = (r * 4 + s) * 64
        return gx[k : k + 64]

    x0 = lane < 32
    x31 = lane >= 992

    def down(v):
        return jnp.where(x0, 0.0, pltpu.roll(v, 32, 1))

    def up_(v):
        return jnp.where(x31, 0.0, pltpu.roll(v, 992, 1))

    qs, ms = [], []
    for r in range(4):
        q0 = blk(r, 1) + jnp.where(y == 0, 0.0, pltpu.roll(blk(r, 3), 1, 1))
        q1 = blk(r, 2) + jnp.where(y == 31, 0.0, pltpu.roll(blk(r, 0), 1023, 1))
        qs.append((q0, q1))
        ms.append(jnp.where(y == 0, blk(r, 0), jnp.where(y == 31, blk(r, 3), 0.0)))
    top = jnp.where(l1 < 32, qs[0][0][:, :128], pltpu.roll(qs[0][1][:, :128], 32, 1))
    low = jnp.where(l1 < 96, pltpu.roll(qs[3][0][:, 896:], 96, 1), qs[3][1][:, 896:])
    rim_tb = jnp.where(l1 < 64, top, low).astype(BF)
    a0 = (ms[1] + down(ms[3])).astype(BF)
    a1 = (ms[2] + up_(ms[0])).astype(BF)
    rim_lr = dot_nt(a0, edge[:, :1024]) + dot_nt(a1, edge[:, 1024:])
    rim_lr = rim_lr.astype(BF)
    for ref in (rim, p1, p2, p3):
        ref[0:64, :] = rim_tb
        ref[64:128, :] = rim_lr
    dl = dot_nt(hd[...], ct[...])
    gbt = dot_nt(pt[...], gp[...])
    packed = []
    for ij in range(9):
        i, j = divmod(ij, 3)
        u = v = None
        for a in range(2):
            k = ((a + i) * 4 + j) * 64
            ua = gbt[k : k + 64, a * 128 : a * 128 + 128]
            va = gbt[k + 64 : k + 128, a * 128 : a * 128 + 128]
            u = ua if u is None else u + ua
            v = va if v is None else v + va
        if ij % 2 == 0:
            packed.append(jnp.where(l1 < 64, u + pltpu.roll(v, 64, 1), 0.0))
        else:
            packed[-1] = jnp.where(l1 < 64, packed[-1], v + pltpu.roll(u, 64, 1))
    for hh in range(2):
        for q in range(5):
            wh[hh * 288 + q * 32 : hh * 288 + q * 32 + 32, :] = packed[q][hh * 32 : hh * 32 + 32]
        for ab in range(4):
            row = hh * 288 + 160 + ab * 32
            wh[row : row + 32, :] = dl[ab * 64 + hh * 32 : ab * 64 + hh * 32 + 32]
    for k, ref in enumerate((wown, p1, p2, p3)):
        ci = (xi + k) & 3
        chunk = jnp.concatenate(
            [wh[pl.ds(al(hh * 288 + ci * 72, 8), 72), :] for hh in range(2)], axis=0
        )
        if k == 0:
            ref[...] = chunk
        else:
            hi, lo = split(chunk)
            ref[128:272, :] = hi
            ref[272:416, :] = lo
    lv_s[...] = dot(lw[...], hd[...]).astype(BF)
    lvk[...] = lv_s[pl.ds(al(h * 64, 64), 64), :]
    lvs[...] = lv_s[pl.ds(al(64 - h * 64, 64), 64), :]
    inner = [
        [
            (qs[1][b] + down(qs[3][b])).astype(BF),
            (qs[2][b] + up_(qs[0][b])).astype(BF),
        ]
        for b in range(2)
    ]
    for g in range(8):
        for a in range(2):
            for b in range(2):
                k = (a * 2 + b) * 128
                xs[g * 64 : g * 64 + 64, k : k + 128] = inner[b][a][:, g * 128 : g * 128 + 128]
    xs[...] = dot_nt(xs[...], perm[...]).astype(BF)
    for g in range(8):
        gxk[:, g * 512 : g * 512 + 512] = xs[pl.ds(al(g * 64 + mine, 32), 32), :]
        gxs[:, g * 512 : g * 512 + 512] = xs[pl.ds(al(g * 64 + other, 32), 32), :]


def bundle_kernel(rim, wown, r1, r2, r3, out, wsum):
    w = wown[...]
    out[0:128, :] = rim[...]
    for k, ref in enumerate((r1, r2, r3)):
        out[(k + 1) * 128 : (k + 2) * 128, :] = ref[0:128, :]
        w = w + (ref[128:272, :].astype(F32) + ref[272:416, :].astype(F32))
    wsum[...] = w
    hi, lo = split(w)
    out[512:656, :] = hi
    out[656:800, :] = lo


def route_rims_kernel(meta, codes, wsum, b0, b1, b2, b3, *rest):
    outs, wk, acc, ws = rest[:8], rest[8], rest[9], rest[10]
    acc[...] = jnp.zeros((1024, 128), F32)
    half = lax.broadcasted_iota(jnp.int32, (32, 128), 1) // 64
    h, lch, zx = meta[24], meta[25], meta[27]
    for bi, bundle in enumerate((b0, b1, b2, b3)):

        @pl.loop(0, 16)
        def _(m, bi=bi, bundle=bundle):
            j = m >> 2
            r = m & 3
            base = (bi * 32 + j * 8 + h * 4 + r) * 3
            t = codes[base]
            s = codes[base + 1]

            @pl.when((t >> 3) == zx)
            def _():
                for hd in range(2):
                    k = ((t & 6) | hd) ^ lch
                    row = al(j * 128 + (r >> 1) * 64 + hd * 32, 32)
                    v = bundle[pl.ds(row, 32), :].astype(F32)
                    dst = al(k * 128 + (t & 1) * 64 + (s >> 1) * 32, 32)
                    place(acc, dst, v, r, s, half)

    w = wsum[...]
    for ref in (b1, b2, b3):
        w = w + (ref[512:656, :].astype(F32) + ref[656:800, :].astype(F32))
    ws[...] = w
    mine = ws[pl.ds(al(h * 72, 8), 72), :]
    far = ws[pl.ds(al(72 - h * 72, 8), 72), :]
    wk[...] = mine
    pieces = []
    for v in (mine, far):
        hi, lo = split(v)
        pieces.append(jnp.concatenate([hi.astype(F32), lo.astype(F32)], axis=0).astype(BF))
    for k in range(8):
        outs[k][0:128, :] = acc[k * 128 : k * 128 + 128, :].astype(BF)
        if k:
            outs[k][128:272, :] = pieces[k & 1]


def final_kernel(
    meta, own, r1, r2, r3, r4, r5, r6, r7, wk, gxk, gxr, lvk, lvr, spread, rev, gin, lev, wout
):
    h = meta[24]
    rets = (r1, r2, r3, r4, r5, r6, r7)
    acc = own[0:128, :].astype(F32)
    w = wk[...]
    for ref in rets:
        acc = acc + ref[0:128, :].astype(F32)
        pieces = ref[128:272, :].astype(F32)
        w = w + (pieces[0:72] + pieces[72:144])
    wout[...] = w
    lane = lax.broadcasted_iota(jnp.int32, (128, 128), 1)
    row = lax.broadcasted_iota(jnp.int32, (128, 128), 0)
    flag = jnp.zeros((128, 128), jnp.int32)
    for tile in range(2):
        for side in range(4):
            f = meta[(tile * 4 + side) * 3 + 2]
            here = ((row >> 5) == tile * 2 + (side >> 1)) & ((lane >> 6) == (side & 1))
            flag = jnp.where(here, f, flag)
    turned = dot(acc.astype(BF), rev[...])
    acc = jnp.where(flag == 1, turned, acc).astype(BF)
    for tile, src in ((h, gxk), (1 - h, gxr)):
        gin[tile] = src[...]
    for tile in range(2):
        st = jnp.concatenate([acc[tile * 64 : tile * 64 + 32], acc[tile * 64 + 32 : tile * 64 + 64]], axis=1)
        delta = dot(st, spread[...])
        gin[tile] = (gin[tile].astype(F32) + delta).astype(BF)
    lev[h] = lvk[...]
    lev[1 - h] = lvr[...]


def unpack_kernel(meta, own, r1, r2, r3, gc, gl, ws):
    xi = meta[26]
    for k, ref in enumerate((own, r1, r2, r3)):
        ws[pl.ds(al(((xi - k) & 3) * 72, 8), 72), :] = ref[...]
    for ij in range(9):
        v = ws[(ij // 2) * 32 : (ij // 2) * 32 + 32, :]
        if ij % 2:
            v = pltpu.roll(v, 64, 1)
        gc[ij] = v[:, :64]
    for ab in range(4):
        gl[ab] = ws[160 + ab * 32 : 192 + ab * 32, :]


def call(kernel, outs, args, smem, scratch=(), name=None):
    specs = [
        pl.BlockSpec(memory_space=pltpu.SMEM if i < smem else pltpu.VMEM) for i in range(len(args))
    ]
    single = not isinstance(outs, list)
    shapes = [outs] if single else outs
    res = pl.pallas_call(
        kernel,
        out_shape=[jax.ShapeDtypeStruct(s, d) for s, d in shapes],
        in_specs=specs,
        out_specs=[pl.BlockSpec(memory_space=pltpu.VMEM) for _ in shapes],
        scratch_shapes=list(scratch),
        compiler_params=pltpu.CompilerParams(vmem_limit_bytes=58 << 20),
        name=name,
    )(*args)
    return res[0] if single else res


def ring(v, axis, k):
    return lax.ppermute(v, axis, [(i, (i + k) % 4) for i in range(4)])


def swap(v):
    return lax.ppermute(v, "h", [(0, 1), (1, 0)])


def octet(v, k):
    return lax.ppermute(v, ("l", "c", "h"), [(i, i ^ k) for i in range(8)])


def on_device(inputs, gluing, conv_weight, level_weight, cotangent):
    perm, edge, rev, spread = constants()
    zi, xi, li, ci, hi = (lax.axis_index(n) for n in ("z", "x", "l", "c", "h"))
    extra = jnp.stack([hi, li * 4 + ci * 2 + hi, xi, zi * 4 + xi]).astype(jnp.int32)
    meta = jnp.concatenate([gluing.reshape(24), extra])

    strips = call(strips_kernel, ((144, 128), BF), (meta, inputs, spread), 1, name="strips")
    got = [ring(strips, "x", k) for k in (1, 2, 3)]
    bundle = jnp.concatenate([strips] + got, axis=0)
    send_in, send_cot = call(
        send_kernel, [((32, 4096), BF), ((64, 1024), BF)], (meta, inputs, cotangent), 1, name="send"
    )
    rin, rcot = swap(send_in), swap(send_cot)
    bundles = [bundle] + [ring(bundle, "z", k) for k in (1, 2, 3)]
    codes = jnp.stack([b.reshape(4, 144, 128)[:, 128, :24] for b in bundles])
    codes = codes.astype(jnp.int32).reshape(384)
    routed = call(
        route_strips_kernel,
        [((64, 128), BF)] * 8,
        (meta, codes, *bundles),
        2,
        [pltpu.VMEM((512, 128), F32)],
        name="route_strips",
    )
    halos = [routed[0]] + [octet(routed[k], k) for k in range(1, 8)]

    w9 = jnp.transpose(conv_weight, (2, 3, 0, 1))
    w9t = jnp.transpose(conv_weight, (2, 3, 1, 0))
    wb, wbt = call(
        weight_kernel, [((256, 1024), BF), ((1024, 256), BF)], (w9, w9t), 0, name="weights"
    )
    lwt = jnp.transpose(level_weight, (2, 3, 1, 0)).reshape(256, 128)
    lw = jnp.transpose(level_weight, (0, 2, 3, 1)).reshape(128, 256)
    gxk, gxs, lvk, lvs, rim, wown, p1, p2, p3 = call(
        main_kernel,
        [
            ((32, 4096), BF), ((32, 4096), BF), ((64, 1024), BF), ((64, 1024), BF), ((128, 128), BF),
            ((144, 128), F32), ((416, 128), BF), ((416, 128), BF), ((416, 128), BF),
        ],
        (meta, inputs, rin, cotangent, rcot, *halos, wb, wbt, lw, lwt, perm, edge, rev),
        1,
        [
            pltpu.VMEM((512, 512), BF), pltpu.VMEM((1024, 1024), BF), pltpu.VMEM((128, 1024), BF),
            pltpu.VMEM((64, 128), F32), pltpu.VMEM((64, 128), F32), pltpu.VMEM((256, 1024), F32),
            pltpu.VMEM((256, 1024), F32), pltpu.VMEM((256, 1024), BF), pltpu.VMEM((256, 1024), BF),
            pltpu.VMEM((576, 128), F32), pltpu.VMEM((128, 1024), BF),
        ],
        name="main",
    )
    back = [ring(p, "x", k) for p, k in ((p1, 1), (p2, 2), (p3, 3))]
    zpay, wsum = call(
        bundle_kernel, [((800, 128), BF), ((144, 128), F32)], (rim, wown, *back), 0, name="bundle"
    )
    zback = [zpay] + [ring(zpay, "z", k) for k in (1, 2, 3)]
    gxr, lvr = swap(gxs), swap(lvs)
    *rets, wk = call(
        route_rims_kernel,
        [((272, 128), BF)] * 8 + [((72, 128), F32)],
        (meta, codes, wsum, *zback),
        2,
        [pltpu.VMEM((1024, 128), F32), pltpu.VMEM((144, 128), F32)],
        name="route_rims",
    )
    rets = [rets[0]] + [octet(rets[k], k) for k in range(1, 8)]
    gin, lev, wpart = call(
        final_kernel,
        [((2, 32, 4096), BF), ((2, 64, 1024), BF), ((72, 128), F32)],
        (meta, *rets, wk, gxk, gxr, lvk, lvr, spread, rev),
        1,
        name="final",
    )
    wall = [wpart] + [ring(wpart, "x", k) for k in (1, 2, 3)]
    gc, gl = call(
        unpack_kernel,
        [((9, 32, 64), F32), ((4, 32, 128), F32)],
        (meta, *wall),
        1,
        [pltpu.VMEM((288, 128), F32)],
        name="unpack",
    )
    grad_conv = jnp.transpose(gc.reshape(3, 3, 32, 64), (3, 2, 0, 1))
    grad_level = jnp.transpose(gl.reshape(2, 2, 32, 128), (3, 2, 0, 1))
    return lev, gin, grad_conv, grad_level


def solution(mesh):
    fine = Mesh(mesh.devices.reshape(4, 4, 2, 2, 2), ("z", "x", "l", "c", "h"))
    tile = ("z", "x", "l", "c")
    return jax.shard_map(
        on_device,
        mesh=fine,
        in_specs=(
            P(tile, "h", None),
            P(tile, None, None),
            P(),
            P(),
            P(tile, "h", None),
        ),
        out_specs=(
            P(tile, "h", None),
            P(tile, "h", None),
            P(None, "h", None, None),
            P(None, "h", None, None),
        ),
        check_vma=False,
    )
```

```python
import functools

import jax
import jax.numpy as jnp
import numpy as np
from jax import lax
from jax.experimental import pallas as pl
from jax.experimental.pallas import tpu as pltpu
from jax.sharding import Mesh
from jax.sharding import PartitionSpec as P

BF = jnp.bfloat16
F32 = jnp.float32
NT = (((1,), (1,)), ((), ()))
SQ = float(np.sqrt(2.0 / np.pi))


def constants():
    perm = np.zeros((512, 512), np.float32)
    for i in range(8):
        for j in range(64):
            perm[i * 64 + j, ((i % 2) * 2 + j % 2) * 128 + (i // 2) * 32 + j // 2] = 1
    edge = np.zeros((128, 2048), np.float32)
    pick = np.zeros((4096, 128), np.float32)
    for side in range(2):
        for a in range(2):
            for x in range(32):
                k = side * 64 + a * 32 + x
                edge[k, a * 1024 + x * 32 + 31 * side] = 1
                pick[(2 * x + a) * 64 + 63 * side, k] = 1
    ends = np.zeros((256, 128), np.float32)
    for b in range(2):
        for y in range(32):
            ends[2 * y + b, b * 32 + y] = 1
            ends[128 + 64 + 2 * y + b, 64 + b * 32 + y] = 1
    rev = np.zeros((128, 128), np.float32)
    for half in range(2):
        for i in range(64):
            rev[half * 64 + i, half * 64 + 63 - i] = 1
    return [jnp.asarray(m, BF) for m in (perm, edge, pick, ends, rev)]


def dot(a, b):
    return jnp.dot(a, b, preferred_element_type=F32)


def dot_nt(a, b):
    return lax.dot_general(a, b, NT, preferred_element_type=F32)


def al(v, m):
    return pl.multiple_of(v, m)


def split(v):
    hi = v.astype(BF)
    return hi, (v - hi.astype(F32)).astype(BF)


def strips_kernel(glue, inp, cot, pick, ends, out, send):
    both = inp[...].reshape(64, 4096)
    lr = dot(both, pick[...]).astype(BF)
    tb = dot(jnp.concatenate([both[:, :128], both[:, 3968:]], axis=1), ends[...]).astype(BF)
    lane = lax.broadcasted_iota(jnp.int32, (16, 128), 1)
    codes = jnp.zeros((16, 128), jnp.int32)
    for tile in range(2):
        for side in range(4):
            t, s = glue[0, tile, side], glue[1, tile, side]
            k = tile * 4 + side
            codes = jnp.where(lane == k, t >> 3, codes)
            codes = jnp.where(lane == k + 8, (t & 7) * 4 + s, codes)
    codes = codes.astype(F32).astype(BF)
    for d in range(16):
        for tile in range(2):
            out[d, tile * 64 : tile * 64 + 32, :] = tb[tile * 32 : tile * 32 + 32]
            out[d, tile * 64 + 32 : tile * 64 + 64, :] = lr[tile * 32 : tile * 32 + 32]
        out[d, 128:144, :] = codes
    o = 1 - lax.axis_index("h")
    send[:, :4096] = inp[o]
    send[:, 4096:5120] = cot[o, :32]
    send[:, 5120:] = cot[o, 32:]


def weight_kernel(w, lwc, wb, wbt, lw, lwt):
    wb[...] = jnp.zeros((256, 1024), BF)
    for a in range(2):
        for b in range(2):
            ab = (a * 2 + b) * 64
            for i in range(3):
                for j in range(3):
                    rs = ((a + i) * 4 + b + j) * 64
                    wb[ab : ab + 64, rs : rs + 64] = w[i, j]
    wbt[...] = wb[...].T
    row = lax.broadcasted_iota(jnp.int32, (256, 256), 0)
    col = lax.broadcasted_iota(jnp.int32, (256, 256), 1)
    order = jnp.where((row & 63) * 4 + (row >> 6) == col, 1.0, 0.0).astype(BF)
    v = dot(order, lwc[...]).astype(BF)
    lwt[...] = v
    lw[...] = v.T


def place(acc, row, v, flip_half, dst_side, half):
    v = pltpu.roll(v, flip_half * 64, 1)
    acc[pl.ds(row, 32), :] = jnp.where(half == (dst_side & 1), v, acc[pl.ds(row, 32), :])


def route_strips_kernel(codes, got, out, acc):
    acc[...] = jnp.zeros((512, 128), F32)
    half = lax.broadcasted_iota(jnp.int32, (32, 128), 1) // 64

    @pl.loop(0, 16)
    def _(i):
        for m in range(8):
            c = codes[i * 8 + m]
            r = m & 3

            @pl.when(c >= 0)
            def _(m=m, c=c, r=r):
                v = got[i, (m >> 1) * 32 : (m >> 1) * 32 + 32, :].astype(F32)
                place(acc, al((c >> 1) * 32, 32), v, (r ^ c) & 1, c, half)

    for k in range(8):
        out[k] = acc[k * 64 : k * 64 + 64, :].astype(BF)


def flip(strips, rev, first, second):
    n = strips.shape[0]
    turned = dot(strips.astype(BF), rev)
    lane = lax.broadcasted_iota(jnp.int32, (n, 128), 1)
    flag = jnp.where(lane < 64, first, second)
    return jnp.where(flag == 1, turned, strips)


def main_kernel(
    glue, inp, rcv, cot, halo, wb, wbt, lw, lwt, perm, edge, rev,
    keep, send, pay,
    xs, pt, ct, pre_s, gh_s, hd, gp, wh, gs, lv_s,
):
    h = lax.axis_index("h")
    mine, other = h * 32, 32 - h * 32
    for g in range(8):
        xs[pl.ds(al(g * 64 + mine, 32), 32), :] = inp[h, :, g * 512 : g * 512 + 512]
        xs[pl.ds(al(g * 64 + other, 32), 32), :] = rcv[:, g * 512 : g * 512 + 512]
    ct[pl.ds(al(h * 64, 64), 64), :] = cot[h]
    ct[pl.ds(al(64 - h * 64, 64), 32), :] = rcv[:, 4096:5120]
    ct[pl.ds(al(96 - h * 64, 32), 32), :] = rcv[:, 5120:]
    nat = dot(xs[...], perm[...])
    ph = [
        [
            jnp.concatenate(
                [nat[g * 64 : g * 64 + 64, (a * 2 + b) * 128 : (a * 2 + b) * 128 + 128] for g in range(8)],
                axis=1,
            )
            for b in range(2)
        ]
        for a in range(2)
    ]
    parts = []
    for q in range(2):
        t = [halo[k].astype(F32) for k in range(q, 8, 2)]
        parts.append((t[0] + t[1]) + (t[2] + t[3]))
    tb, lr = (
        jnp.concatenate([parts[0][k : k + 32], parts[1][k : k + 32]], axis=0) for k in (0, 32)
    )
    fl = [glue[2, h, s] for s in range(4)]
    tb = flip(tb, rev[...], fl[0], fl[1])
    lr = flip(lr, rev[...], fl[2], fl[3])
    sp = dot(lr.astype(BF), edge[...])
    lane = lax.broadcasted_iota(jnp.int32, (64, 1024), 1)
    y = lane & 31
    l1 = lax.broadcasted_iota(jnp.int32, (64, 128), 1)
    cols = [[None] * 4 for _ in range(2)]
    for a in range(2):
        spa = sp[:, a * 1024 : a * 1024 + 1024]
        cols[a][0] = jnp.where(y == 0, spa, pltpu.roll(ph[a][1], 1, 1))
        cols[a][1] = ph[a][0]
        cols[a][2] = ph[a][1]
        cols[a][3] = jnp.where(y == 31, spa, pltpu.roll(ph[a][0], 1023, 1))
    top_shift = (97, 0, 96, 127)
    low_shift = (1, 32, 0, 31)
    for s in range(4):
        pt[(4 + s) * 64 : (4 + s) * 64 + 64, :] = cols[0][s].astype(BF)
        pt[(8 + s) * 64 : (8 + s) * 64 + 64, :] = cols[1][s].astype(BF)
        up = pltpu.roll(cols[1][s], 32, 1)
        t = pltpu.roll(tb, top_shift[s], 1) if top_shift[s] else tb
        if s == 0:
            t = jnp.where(l1 == 0, 0.0, t)
        if s == 3:
            t = jnp.where(l1 == 31, 0.0, t)
        pt[s * 64 : s * 64 + 64, 128:] = up[:, 128:].astype(BF)
        pt[s * 64 : s * 64 + 64, :128] = jnp.where(l1 < 32, t, up[:, :128]).astype(BF)
        dn = pltpu.roll(cols[0][s], 992, 1)
        t = pltpu.roll(tb, low_shift[s], 1) if low_shift[s] else tb
        if s == 0:
            t = jnp.where(l1 == 96, 0.0, t)
        if s == 3:
            t = jnp.where(l1 == 127, 0.0, t)
        pt[(12 + s) * 64 : (12 + s) * 64 + 64, :896] = dn[:, :896].astype(BF)
        pt[(12 + s) * 64 : (12 + s) * 64 + 64, 896:] = jnp.where(l1 >= 96, t, dn[:, 896:]).astype(BF)
    pre_s[...] = dot(wb[...], pt[...])
    gh_s[...] = dot(lwt[...], ct[...])
    for q in range(8):
        rows = slice(q * 32, q * 32 + 32)
        v = pre_s[rows, :]
        v2 = v * v
        th = jnp.tanh(SQ * (v + 0.044715 * (v2 * v)))
        half = 0.5 * (1.0 + th)
        hd[rows, :] = (v * half).astype(BF)
        d = half + 0.5 * v * (1.0 - th * th) * (SQ * (1.0 + 3 * 0.044715 * v2))
        gp[rows, :] = (gh_s[rows, :] * d).astype(BF)
    gx = dot(wbt[...], gp[...])

    def blk(r, s):
        k = (r * 4 + s) * 64
        return gx[k : k + 64]

    x0 = lane < 32
    x31 = lane >= 992

    def down(v):
        return jnp.where(x0, 0.0, pltpu.roll(v, 32, 1))

    def up_(v):
        return jnp.where(x31, 0.0, pltpu.roll(v, 992, 1))

    qs, ms = [], []
    for r in range(4):
        q0 = blk(r, 1) + jnp.where(y == 0, 0.0, pltpu.roll(blk(r, 3), 1, 1))
        q1 = blk(r, 2) + jnp.where(y == 31, 0.0, pltpu.roll(blk(r, 0), 1023, 1))
        qs.append((q0, q1))
        ms.append(jnp.where(y == 0, blk(r, 0), jnp.where(y == 31, blk(r, 3), 0.0)))
    top = jnp.where(l1 < 32, qs[0][0][:, :128], pltpu.roll(qs[0][1][:, :128], 32, 1))
    low = jnp.where(l1 < 96, pltpu.roll(qs[3][0][:, 896:], 96, 1), qs[3][1][:, 896:])
    rim_tb = jnp.where(l1 < 64, top, low).astype(BF)
    a0 = (ms[1] + down(ms[3])).astype(BF)
    a1 = (ms[2] + up_(ms[0])).astype(BF)
    rim_lr = dot_nt(a0, edge[:, :1024]) + dot_nt(a1, edge[:, 1024:])
    rim_lr = rim_lr.astype(BF)
    for d in range(16):
        pay[d, 0:64, :] = rim_tb
        pay[d, 64:128, :] = rim_lr
    dl = dot_nt(hd[...], ct[...])
    gbt = dot_nt(pt[...], gp[...])
    packed = []
    for ij in range(9):
        i, j = divmod(ij, 3)
        u = v = None
        for a in range(2):
            k = ((a + i) * 4 + j) * 64
            ua = gbt[k : k + 64, a * 128 : a * 128 + 128]
            va = gbt[k + 64 : k + 128, a * 128 : a * 128 + 128]
            u = ua if u is None else u + ua
            v = va if v is None else v + va
        if ij % 2 == 0:
            packed.append(jnp.where(l1 < 64, u + pltpu.roll(v, 64, 1), 0.0))
        else:
            packed[-1] = jnp.where(l1 < 64, packed[-1], v + pltpu.roll(u, 64, 1))
    for hh in range(2):
        base = hh * 384
        for q in range(5):
            wh[base + q * 32 : base + q * 32 + 32, :] = packed[q][hh * 32 : hh * 32 + 32]
        for ab in range(4):
            row = base + 160 + ab * 32
            wh[row : row + 32, :] = dl[ab * 64 + hh * 32 : ab * 64 + hh * 32 + 32]
        wh[base + 288 : base + 384, :] = jnp.zeros((96, 128), F32)
    for d in range(16):
        chunk = jnp.concatenate([wh[d * 24 : d * 24 + 24, :], wh[384 + d * 24 : 408 + d * 24, :]], axis=0)
        hi, lo = split(chunk)
        pay[d, 128:176, :] = hi
        pay[d, 176:224, :] = lo
    lv_s[...] = dot(lw[...], hd[...]).astype(BF)
    for b in range(2):
        gs[:, b * 1024 : b * 1024 + 1024] = (qs[1][b] + down(qs[3][b])).astype(BF)
        gs[:, 2048 + b * 1024 : 3072 + b * 1024] = (qs[2][b] + up_(qs[0][b])).astype(BF)
    for ref, row in ((keep, h * 32), (send, 32 - h * 32)):
        ref[:, :4096] = gs[pl.ds(al(row, 32), 32), :]
        ref[:, 4096:5120] = lv_s[pl.ds(al(row * 2, 64), 32), :]
        ref[:, 5120:] = lv_s[pl.ds(al(row * 2 + 32, 32), 32), :]


def route_rims_kernel(codes, got, out, acc):
    acc[...] = jnp.zeros((1024, 128), F32)
    half = lax.broadcasted_iota(jnp.int32, (32, 128), 1) // 64
    h = lax.axis_index("h")

    @pl.loop(0, 16)
    def _(i):
        for r in range(4):
            c = codes[i * 8 + h * 4 + r]

            @pl.when(c >= 0)
            def _(c=c, r=r):
                t, s = c >> 2, c & 3
                for hh in range(2):
                    row = (r >> 1) * 64 + hh * 32
                    v = got[i, row : row + 32, :].astype(F32)
                    dst = ((t & 6) | hh) * 128 + (t & 1) * 64 + (s >> 1) * 32
                    place(acc, al(dst, 32), v, (r ^ s) & 1, s, half)

    w = None
    for i in range(16):
        v = got[i, 128:176, :].astype(F32) + got[i, 176:224, :].astype(F32)
        w = v if w is None else w + v
    pieces = []
    for q in range(2):
        hi, lo = split(w[q * 24 : q * 24 + 24])
        pieces.append(jnp.concatenate([hi.astype(F32), lo.astype(F32)], axis=0).astype(BF))
    for k in range(8):
        out[k, 0:128, :] = acc[k * 128 : k * 128 + 128, :].astype(BF)
        out[k, 128:176, :] = pieces[k & 1]


def final_kernel(glue, ret, keep, rcv, perm, edge, rev, gin, lev, wout, gs, xs):
    h = lax.axis_index("h")
    acc = w = None
    for k in range(8):
        v = ret[k, 0:128, :].astype(F32)
        p = ret[k, 128:176, :].astype(F32)
        p = p[0:24] + p[24:48]
        acc = v if acc is None else acc + v
        w = p if w is None else w + p
    for d in range(16):
        wout[d] = w
    lane = lax.broadcasted_iota(jnp.int32, (128, 128), 1)
    row = lax.broadcasted_iota(jnp.int32, (128, 128), 0)
    flag = jnp.zeros((128, 128), jnp.int32)
    for tile in range(2):
        for side in range(4):
            here = ((row >> 5) == tile * 2 + (side >> 1)) & ((lane >> 6) == (side & 1))
            flag = jnp.where(here, glue[2, tile, side], flag)
    turned = dot(acc.astype(BF), rev[...])
    acc = jnp.where(flag == 1, turned, acc)
    tb = jnp.concatenate([acc[0:32], acc[64:96]], axis=0)
    lr = jnp.concatenate([acc[32:64], acc[96:128]], axis=0)
    sp = dot(lr.astype(BF), edge[...])
    gs[pl.ds(al(h * 32, 32), 32), :] = keep[:, :4096]
    gs[pl.ds(al(32 - h * 32, 32), 32), :] = rcv[:, :4096]
    y = lax.broadcasted_iota(jnp.int32, (64, 1024), 1) & 31
    l1 = lax.broadcasted_iota(jnp.int32, (64, 128), 1)
    for a in range(2):
        for b in range(2):
            ab = a * 2 + b
            v = gs[:, ab * 1024 : ab * 1024 + 1024].astype(F32)
            v = v + jnp.where(y == 31 * b, sp[:, a * 1024 : a * 1024 + 1024], 0.0)
            shift = ((0, 96), (32, 0))[a][b]
            t = pltpu.roll(tb, shift, 1) if shift else tb
            t = jnp.where((l1 >= 96) if a else (l1 < 32), t, 0.0)
            for g in range(8):
                part = v[:, g * 128 : g * 128 + 128]
                if g == 7 * a:
                    part = part + t
                xs[g * 64 : g * 64 + 64, ab * 128 : ab * 128 + 128] = part.astype(BF)
    nat = dot_nt(xs[...], perm[...]).astype(BF)
    for g in range(8):
        for tile in range(2):
            k = g * 64 + tile * 32
            gin[tile, :, g * 512 : g * 512 + 512] = nat[k : k + 32]
    for tile, src in ((h, keep), (1 - h, rcv)):
        lev[tile, :32] = src[:, 4096:5120]
        lev[tile, 32:] = src[:, 5120:]


def unpack_kernel(ws, gc, gl):
    w = ws[...].reshape(384, 128)
    for ij in range(9):
        v = w[(ij // 2) * 32 : (ij // 2) * 32 + 32, :]
        if ij % 2:
            v = pltpu.roll(v, 64, 1)
        gc[ij] = v[:, :64]
    for ab in range(4):
        gl[ab] = w[160 + ab * 32 : 192 + ab * 32, :]


def call(kernel, outs, args, smem, scratch=(), name=None):
    specs = [
        pl.BlockSpec(memory_space=pltpu.SMEM if i < smem else pltpu.VMEM) for i in range(len(args))
    ]
    single = not isinstance(outs, list)
    shapes = [outs] if single else outs
    res = pl.pallas_call(
        kernel,
        out_shape=[jax.ShapeDtypeStruct(s, d) for s, d in shapes],
        in_specs=specs,
        out_specs=[pl.BlockSpec(memory_space=pltpu.VMEM) for _ in shapes],
        scratch_shapes=list(scratch),
        compiler_params=pltpu.CompilerParams(vmem_limit_bytes=58 << 20),
        name=name,
    )(*args)
    return res[0] if single else res


def swap(v):
    return lax.ppermute(v, "h", [(0, 1), (1, 0)])


def plane(v):
    return lax.all_to_all(v, ("z", "x"), 0, 0)


def octet(v):
    return lax.all_to_all(v, ("l", "c", "h"), 0, 0)


def on_device(inputs, gluing, conv_weight, level_weight, cotangent):
    perm, edge, pick, ends, rev = constants()
    glue = jnp.transpose(gluing, (2, 0, 1))
    strips, send = call(
        strips_kernel,
        [((16, 144, 128), BF), ((32, 6144), BF)],
        (glue, inputs, cotangent, pick, ends),
        1,
        name="strips",
    )
    rcv = swap(send)
    got = plane(strips)
    here = (lax.axis_index("z") * 4 + lax.axis_index("x")).astype(BF)
    codes = jnp.where(got[:, 128, :8] == here, got[:, 128, 8:16], -1).astype(jnp.int32).reshape(128)
    routed = call(
        route_strips_kernel,
        ((8, 64, 128), BF),
        (codes, got),
        1,
        [pltpu.VMEM((512, 128), F32)],
        name="route_strips",
    )
    halos = octet(routed)
    w9 = jnp.transpose(conv_weight, (2, 3, 0, 1))
    lwc = jnp.transpose(level_weight, (1, 2, 3, 0)).reshape(256, 128)
    wb, wbt, lw, lwt = call(
        weight_kernel,
        [((256, 1024), BF), ((1024, 256), BF), ((128, 256), BF), ((256, 128), BF)],
        (w9, lwc),
        0,
        name="weights",
    )
    keep, back, pay = call(
        main_kernel,
        [((32, 6144), BF), ((32, 6144), BF), ((16, 224, 128), BF)],
        (glue, inputs, rcv, cotangent, halos, wb, wbt, lw, lwt, perm, edge, rev),
        1,
        [
            pltpu.VMEM((512, 512), BF), pltpu.VMEM((1024, 1024), BF), pltpu.VMEM((128, 1024), BF),
            pltpu.VMEM((256, 1024), F32), pltpu.VMEM((256, 1024), F32), pltpu.VMEM((256, 1024), BF),
            pltpu.VMEM((256, 1024), BF), pltpu.VMEM((768, 128), F32), pltpu.VMEM((64, 4096), BF),
            pltpu.VMEM((128, 1024), BF),
        ],
        name="main",
    )
    rback = swap(back)
    rims = plane(pay)
    outgoing = call(
        route_rims_kernel,
        ((8, 176, 128), BF),
        (codes, rims),
        1,
        [pltpu.VMEM((1024, 128), F32)],
        name="route_rims",
    )
    ret = octet(outgoing)
    gin, lev, wrep = call(
        final_kernel,
        [((2, 32, 4096), BF), ((2, 64, 1024), BF), ((16, 24, 128), F32)],
        (glue, ret, keep, rback, perm, edge, rev),
        1,
        [pltpu.VMEM((64, 4096), BF), pltpu.VMEM((512, 512), BF)],
        name="final",
    )
    wall = plane(wrep)
    gc, gl = call(
        unpack_kernel, [((9, 32, 64), F32), ((4, 32, 128), F32)], (wall,), 0, name="unpack"
    )
    grad_conv = jnp.transpose(gc.reshape(3, 3, 32, 64), (3, 2, 0, 1))
    grad_level = jnp.transpose(gl.reshape(2, 2, 32, 128), (3, 2, 0, 1))
    return lev, gin, grad_conv, grad_level


def solution(mesh):
    fine = Mesh(mesh.devices.reshape(4, 4, 2, 2, 2), ("z", "x", "l", "c", "h"))
    tile = ("z", "x", "l", "c")
    return jax.shard_map(
        on_device,
        mesh=fine,
        in_specs=(
            P(tile, "h", None),
            P(tile, None, None),
            P(),
            P(),
            P(tile, "h", None),
        ),
        out_specs=(
            P(tile, "h", None),
            P(tile, "h", None),
            P(None, "h", None, None),
            P(None, "h", None, None),
        ),
        check_vma=False,
    )
```

```python
import functools

import jax
import jax.numpy as jnp
import numpy as np
from jax import lax
from jax.experimental import pallas as pl
from jax.experimental.pallas import tpu as pltpu
from jax.sharding import Mesh
from jax.sharding import PartitionSpec as P

BF = jnp.bfloat16
F32 = jnp.float32
NT = (((1,), (1,)), ((), ()))
SQ = float(np.sqrt(2.0 / np.pi))


def constants():
    perm = np.zeros((512, 512), np.float32)
    for i in range(8):
        for j in range(64):
            perm[i * 64 + j, ((i % 2) * 2 + j % 2) * 128 + (i // 2) * 32 + j // 2] = 1
    edge = np.zeros((128, 2048), np.float32)
    pick = np.zeros((4096, 128), np.float32)
    for side in range(2):
        for a in range(2):
            for x in range(32):
                k = side * 64 + a * 32 + x
                edge[k, a * 1024 + x * 32 + 31 * side] = 1
                pick[(2 * x + a) * 64 + 63 * side, k] = 1
    ends = np.zeros((256, 128), np.float32)
    for b in range(2):
        for y in range(32):
            ends[2 * y + b, b * 32 + y] = 1
            ends[128 + 64 + 2 * y + b, 64 + b * 32 + y] = 1
    rev = np.zeros((128, 128), np.float32)
    for half in range(2):
        for i in range(64):
            rev[half * 64 + i, half * 64 + 63 - i] = 1
    return [jnp.asarray(m, BF) for m in (perm, edge, pick, ends, rev)]


def dot(a, b):
    return jnp.dot(a, b, preferred_element_type=F32)


def dot_nt(a, b):
    return lax.dot_general(a, b, NT, preferred_element_type=F32)


def al(v, m):
    return pl.multiple_of(v, m)


def strips_kernel(glue, inp, cot, pick, ends, out, send):
    pix = inp[...].reshape(64, 4096)
    lr = dot(pix, pick[...]).astype(BF)
    tb = dot(jnp.concatenate([pix[:, :128], pix[:, 3968:]], axis=1), ends[...]).astype(BF)
    lane = lax.broadcasted_iota(jnp.int32, (16, 128), 1)
    codes = jnp.zeros((16, 128), jnp.int32)
    for tile in range(2):
        for side in range(4):
            t, s = glue[0, tile, side], glue[1, tile, side]
            k = tile * 4 + side
            codes = jnp.where(lane == k, t >> 3, codes)
            codes = jnp.where(lane == k + 8, (t & 7) * 4 + s, codes)
    codes = codes.astype(F32).astype(BF)
    for d in range(16):
        for tile in range(2):
            out[d, tile * 64 : tile * 64 + 32, :] = tb[tile * 32 : tile * 32 + 32]
            out[d, tile * 64 + 32 : tile * 64 + 64, :] = lr[tile * 32 : tile * 32 + 32]
        out[d, 128:144, :] = codes
    o = 1 - lax.axis_index("h")
    send[:, :4096] = inp[o]
    send[:, 4096:5120] = cot[o, :32]
    send[:, 5120:] = cot[o, 32:]


def weight_kernel(w, lwc, wb, wbt, lw, lwt):
    wb[...] = jnp.zeros((256, 1024), BF)
    for a in range(2):
        for b in range(2):
            ab = (a * 2 + b) * 64
            for i in range(3):
                for j in range(3):
                    rs = ((a + i) * 4 + b + j) * 64
                    wb[ab : ab + 64, rs : rs + 64] = w[i, j]
    wbt[...] = wb[...].T
    row = lax.broadcasted_iota(jnp.int32, (256, 256), 0)
    col = lax.broadcasted_iota(jnp.int32, (256, 256), 1)
    order = jnp.where((row & 63) * 4 + (row >> 6) == col, 1.0, 0.0).astype(BF)
    v = dot(order, lwc[...]).astype(BF)
    lwt[...] = v
    lw[...] = v.T


def place(acc, row, v, flip_half, dst_side, half):
    v = pltpu.roll(v, flip_half * 64, 1)
    acc[pl.ds(row, 32), :] = jnp.where(half == (dst_side & 1), v, acc[pl.ds(row, 32), :])


def route_strips_kernel(codes, got, out, acc):
    acc[...] = jnp.zeros((512, 128), F32)
    half = lax.broadcasted_iota(jnp.int32, (32, 128), 1) // 64

    @pl.loop(0, 16)
    def _(i):
        for m in range(8):
            c = codes[i * 8 + m]
            r = m & 3

            @pl.when(c >= 0)
            def _(m=m, c=c, r=r):
                v = got[i, (m >> 1) * 32 : (m >> 1) * 32 + 32, :].astype(F32)
                place(acc, al((c >> 1) * 32, 32), v, (r ^ c) & 1, c, half)

    for k in range(8):
        out[k] = acc[k * 64 : k * 64 + 64, :].astype(BF)


def flip(strips, rev, first, second):
    n = strips.shape[0]
    turned = dot(strips.astype(BF), rev)
    lane = lax.broadcasted_iota(jnp.int32, (n, 128), 1)
    flag = jnp.where(lane < 64, first, second)
    return jnp.where(flag == 1, turned, strips)


def main_kernel(
    glue, inp, rcv, cot, halo, wb, wbt, lw, lwt, perm, edge, rev,
    keep, send, pay, c0, c1, c2, c3, c4, c5, c6, c7,
    xs, pt, ct, pre_s, gh_s, hd, gp, wh, gs, lv_s,
):
    h = lax.axis_index("h")
    mine, other = h * 32, 32 - h * 32
    for g in range(8):
        xs[pl.ds(al(g * 64 + mine, 32), 32), :] = inp[h, :, g * 512 : g * 512 + 512]
        xs[pl.ds(al(g * 64 + other, 32), 32), :] = rcv[:, g * 512 : g * 512 + 512]
    ct[pl.ds(al(h * 64, 64), 64), :] = cot[h]
    ct[pl.ds(al(64 - h * 64, 64), 32), :] = rcv[:, 4096:5120]
    ct[pl.ds(al(96 - h * 64, 32), 32), :] = rcv[:, 5120:]
    nat = dot(xs[...], perm[...])
    ph = [
        [
            jnp.concatenate(
                [nat[g * 64 : g * 64 + 64, (a * 2 + b) * 128 : (a * 2 + b) * 128 + 128] for g in range(8)],
                axis=1,
            )
            for b in range(2)
        ]
        for a in range(2)
    ]
    parts = []
    for q in range(2):
        t = [halo[k].astype(F32) for k in range(q, 8, 2)]
        parts.append((t[0] + t[1]) + (t[2] + t[3]))
    tb, lr = (
        jnp.concatenate([parts[0][k : k + 32], parts[1][k : k + 32]], axis=0) for k in (0, 32)
    )
    fl = [glue[2, h, s] for s in range(4)]
    tb = flip(tb, rev[...], fl[0], fl[1])
    lr = flip(lr, rev[...], fl[2], fl[3])
    sp = dot(lr.astype(BF), edge[...])
    lane = lax.broadcasted_iota(jnp.int32, (64, 1024), 1)
    y = lane & 31
    l1 = lax.broadcasted_iota(jnp.int32, (64, 128), 1)
    cols = [[None] * 4 for _ in range(2)]
    for a in range(2):
        spa = sp[:, a * 1024 : a * 1024 + 1024]
        cols[a][0] = jnp.where(y == 0, spa, pltpu.roll(ph[a][1], 1, 1))
        cols[a][1] = ph[a][0]
        cols[a][2] = ph[a][1]
        cols[a][3] = jnp.where(y == 31, spa, pltpu.roll(ph[a][0], 1023, 1))
    top_shift = (97, 0, 96, 127)
    low_shift = (1, 32, 0, 31)
    for s in range(4):
        pt[(4 + s) * 64 : (4 + s) * 64 + 64, :] = cols[0][s].astype(BF)
        pt[(8 + s) * 64 : (8 + s) * 64 + 64, :] = cols[1][s].astype(BF)
        up = pltpu.roll(cols[1][s], 32, 1)
        t = pltpu.roll(tb, top_shift[s], 1) if top_shift[s] else tb
        if s == 0:
            t = jnp.where(l1 == 0, 0.0, t)
        if s == 3:
            t = jnp.where(l1 == 31, 0.0, t)
        pt[s * 64 : s * 64 + 64, 128:] = up[:, 128:].astype(BF)
        pt[s * 64 : s * 64 + 64, :128] = jnp.where(l1 < 32, t, up[:, :128]).astype(BF)
        dn = pltpu.roll(cols[0][s], 992, 1)
        t = pltpu.roll(tb, low_shift[s], 1) if low_shift[s] else tb
        if s == 0:
            t = jnp.where(l1 == 96, 0.0, t)
        if s == 3:
            t = jnp.where(l1 == 127, 0.0, t)
        pt[(12 + s) * 64 : (12 + s) * 64 + 64, :896] = dn[:, :896].astype(BF)
        pt[(12 + s) * 64 : (12 + s) * 64 + 64, 896:] = jnp.where(l1 >= 96, t, dn[:, 896:]).astype(BF)
    pre_s[...] = dot(wb[...], pt[...])
    gh_s[...] = dot(lwt[...], ct[...])
    for q in range(8):
        rows = slice(q * 32, q * 32 + 32)
        v = pre_s[rows, :]
        v2 = v * v
        th = jnp.tanh(SQ * (v + 0.044715 * (v2 * v)))
        half = 0.5 * (1.0 + th)
        hd[rows, :] = (v * half).astype(BF)
        d = half + 0.5 * v * (1.0 - th * th) * (SQ * (1.0 + 3 * 0.044715 * v2))
        gp[rows, :] = (gh_s[rows, :] * d).astype(BF)
    gx = dot(wbt[...], gp[...])

    def blk(r, s):
        k = (r * 4 + s) * 64
        return gx[k : k + 64]

    x0 = lane < 32
    x31 = lane >= 992

    def down(v):
        return jnp.where(x0, 0.0, pltpu.roll(v, 32, 1))

    def up_(v):
        return jnp.where(x31, 0.0, pltpu.roll(v, 992, 1))

    qs, ms = [], []
    for r in range(4):
        q0 = blk(r, 1) + jnp.where(y == 0, 0.0, pltpu.roll(blk(r, 3), 1, 1))
        q1 = blk(r, 2) + jnp.where(y == 31, 0.0, pltpu.roll(blk(r, 0), 1023, 1))
        qs.append((q0, q1))
        ms.append(jnp.where(y == 0, blk(r, 0), jnp.where(y == 31, blk(r, 3), 0.0)))
    top = jnp.where(l1 < 32, qs[0][0][:, :128], pltpu.roll(qs[0][1][:, :128], 32, 1))
    low = jnp.where(l1 < 96, pltpu.roll(qs[3][0][:, 896:], 96, 1), qs[3][1][:, 896:])
    rim_tb = jnp.where(l1 < 64, top, low).astype(BF)
    a0 = (ms[1] + down(ms[3])).astype(BF)
    a1 = (ms[2] + up_(ms[0])).astype(BF)
    rim_lr = dot_nt(a0, edge[:, :1024]) + dot_nt(a1, edge[:, 1024:])
    rim_lr = rim_lr.astype(BF)
    for d in range(16):
        pay[d, 0:64, :] = rim_tb
        pay[d, 64:128, :] = rim_lr
    dl = dot_nt(hd[...], ct[...])
    gbt = dot_nt(pt[...], gp[...])
    packed = []
    for ij in range(9):
        i, j = divmod(ij, 3)
        u = v = None
        for a in range(2):
            k = ((a + i) * 4 + j) * 64
            ua = gbt[k : k + 64, a * 128 : a * 128 + 128]
            va = gbt[k + 64 : k + 128, a * 128 : a * 128 + 128]
            u = ua if u is None else u + ua
            v = va if v is None else v + va
        if ij % 2 == 0:
            packed.append(jnp.where(l1 < 64, u + pltpu.roll(v, 64, 1), 0.0))
        else:
            packed[-1] = jnp.where(l1 < 64, packed[-1], v + pltpu.roll(u, 64, 1))
    for hh in range(2):
        base = hh * 288
        for q in range(5):
            wh[base + q * 32 : base + q * 32 + 32, :] = packed[q][hh * 32 : hh * 32 + 32]
        for ab in range(4):
            row = base + 160 + ab * 32
            wh[row : row + 32, :] = dl[ab * 64 + hh * 32 : ab * 64 + hh * 32 + 32]
    lch = lax.axis_index("l") * 4 + lax.axis_index("c") * 2 + h
    for k, ref in enumerate((c0, c1, c2, c3, c4, c5, c6, c7)):
        d = lch ^ k
        ref[...] = wh[pl.ds(al((d & 1) * 288 + (d >> 1) * 72, 8), 72), :]
    lv_s[...] = dot(lw[...], hd[...]).astype(BF)
    for b in range(2):
        gs[:, b * 1024 : b * 1024 + 1024] = (qs[1][b] + down(qs[3][b])).astype(BF)
        gs[:, 2048 + b * 1024 : 3072 + b * 1024] = (qs[2][b] + up_(qs[0][b])).astype(BF)
    for ref, row in ((keep, h * 32), (send, 32 - h * 32)):
        ref[:, :4096] = gs[pl.ds(al(row, 32), 32), :]
        ref[:, 4096:5120] = lv_s[pl.ds(al(row * 2, 64), 32), :]
        ref[:, 5120:] = lv_s[pl.ds(al(row * 2 + 32, 32), 32), :]


def route_rims_kernel(codes, got, out, acc):
    acc[...] = jnp.zeros((1024, 128), F32)
    half = lax.broadcasted_iota(jnp.int32, (32, 128), 1) // 64
    h = lax.axis_index("h")

    @pl.loop(0, 16)
    def _(i):
        for r in range(4):
            c = codes[i * 8 + h * 4 + r]

            @pl.when(c >= 0)
            def _(c=c, r=r):
                t, s = c >> 2, c & 3
                for hh in range(2):
                    row = (r >> 1) * 64 + hh * 32
                    v = got[i, row : row + 32, :].astype(F32)
                    dst = ((t & 6) | hh) * 128 + (t & 1) * 64 + (s >> 1) * 32
                    place(acc, al(dst, 32), v, (r ^ s) & 1, s, half)

    for k in range(8):
        out[k] = acc[k * 128 : k * 128 + 128, :].astype(BF)


def final_kernel(glue, ret, keep, rcv, perm, edge, rev, gin, lev, gs, xs):
    h = lax.axis_index("h")
    acc = ret[0].astype(F32)
    for k in range(1, 8):
        acc = acc + ret[k].astype(F32)
    lane = lax.broadcasted_iota(jnp.int32, (128, 128), 1)
    row = lax.broadcasted_iota(jnp.int32, (128, 128), 0)
    flag = jnp.zeros((128, 128), jnp.int32)
    for tile in range(2):
        for side in range(4):
            here = ((row >> 5) == tile * 2 + (side >> 1)) & ((lane >> 6) == (side & 1))
            flag = jnp.where(here, glue[2, tile, side], flag)
    turned = dot(acc.astype(BF), rev[...])
    acc = jnp.where(flag == 1, turned, acc)
    tb = jnp.concatenate([acc[0:32], acc[64:96]], axis=0)
    lr = jnp.concatenate([acc[32:64], acc[96:128]], axis=0)
    sp = dot(lr.astype(BF), edge[...])
    gs[pl.ds(al(h * 32, 32), 32), :] = keep[:, :4096]
    gs[pl.ds(al(32 - h * 32, 32), 32), :] = rcv[:, :4096]
    y = lax.broadcasted_iota(jnp.int32, (64, 1024), 1) & 31
    l1 = lax.broadcasted_iota(jnp.int32, (64, 128), 1)
    for a in range(2):
        for b in range(2):
            ab = a * 2 + b
            v = gs[:, ab * 1024 : ab * 1024 + 1024].astype(F32)
            v = v + jnp.where(y == 31 * b, sp[:, a * 1024 : a * 1024 + 1024], 0.0)
            shift = ((0, 96), (32, 0))[a][b]
            t = pltpu.roll(tb, shift, 1) if shift else tb
            t = jnp.where((l1 >= 96) if a else (l1 < 32), t, 0.0)
            for g in range(8):
                part = v[:, g * 128 : g * 128 + 128]
                if g == 7 * a:
                    part = part + t
                xs[g * 64 : g * 64 + 64, ab * 128 : ab * 128 + 128] = part.astype(BF)
    nat = dot_nt(xs[...], perm[...]).astype(BF)
    for g in range(8):
        for tile in range(2):
            k = g * 64 + tile * 32
            gin[tile, :, g * 512 : g * 512 + 512] = nat[k : k + 32]
    for tile, src in ((h, keep), (1 - h, rcv)):
        lev[tile, :32] = src[:, 4096:5120]
        lev[tile, 32:] = src[:, 5120:]


def unpack_kernel(w0, w1, w2, w3, gc, gl, w):
    q = lax.axis_index("l") * 2 + lax.axis_index("c")
    for k, ref in enumerate((w0, w1, w2, w3)):
        w[pl.ds(al((q ^ k) * 72, 8), 72), :] = ref[...]
    for ij in range(9):
        v = w[(ij // 2) * 32 : (ij // 2) * 32 + 32, :]
        if ij % 2:
            v = pltpu.roll(v, 64, 1)
        gc[ij] = v[:, :64]
    for ab in range(4):
        gl[:, ab // 2, ab % 2, :] = w[160 + ab * 32 : 192 + ab * 32, :]


def call(kernel, outs, args, smem, scratch=(), name=None):
    specs = [
        pl.BlockSpec(memory_space=pltpu.SMEM if i < smem else pltpu.VMEM) for i in range(len(args))
    ]
    single = not isinstance(outs, list)
    shapes = [outs] if single else outs
    res = pl.pallas_call(
        kernel,
        out_shape=[jax.ShapeDtypeStruct(s, d) for s, d in shapes],
        in_specs=specs,
        out_specs=[pl.BlockSpec(memory_space=pltpu.VMEM) for _ in shapes],
        scratch_shapes=list(scratch),
        compiler_params=pltpu.CompilerParams(vmem_limit_bytes=58 << 20),
        name=name,
    )(*args)
    return res[0] if single else res


def swap(v):
    return lax.ppermute(v, "h", [(0, 1), (1, 0)])


def hop(v, axes, n, k):
    return lax.ppermute(v, axes, [(i, i ^ k) for i in range(n)]) if k else v


def ring(v, axis, k):
    return lax.ppermute(v, axis, [(i, (i + k) % 4) for i in range(4)]) if k else v


def total(parts):
    while len(parts) > 1:
        parts = [a + b for a, b in zip(parts[::2], parts[1::2])]
    return parts[0]


def plane(v):
    return lax.all_to_all(v, ("z", "x"), 0, 0)


def octet(v):
    return lax.all_to_all(v, ("l", "c", "h"), 0, 0)


def on_device(inputs, gluing, conv_weight, level_weight, cotangent):
    perm, edge, pick, ends, rev = constants()
    glue = jnp.transpose(gluing, (2, 0, 1))
    strips, send = call(
        strips_kernel,
        [((16, 144, 128), BF), ((32, 6144), BF)],
        (glue, inputs, cotangent, pick, ends),
        1,
        name="strips",
    )
    rcv = swap(send)
    got = plane(strips)
    here = (lax.axis_index("z") * 4 + lax.axis_index("x")).astype(BF)
    codes = jnp.where(got[:, 128, :8] == here, got[:, 128, 8:16], -1).astype(jnp.int32).reshape(128)
    routed = call(
        route_strips_kernel,
        ((8, 64, 128), BF),
        (codes, got),
        1,
        [pltpu.VMEM((512, 128), F32)],
        name="route_strips",
    )
    halos = octet(routed)
    w9 = jnp.transpose(conv_weight, (2, 3, 0, 1))
    lwc = jnp.transpose(level_weight, (1, 2, 3, 0)).reshape(256, 128)
    wb, wbt, lw, lwt = call(
        weight_kernel,
        [((256, 1024), BF), ((1024, 256), BF), ((128, 256), BF), ((256, 128), BF)],
        (w9, lwc),
        0,
        name="weights",
    )
    keep, back, pay, *chunks = call(
        main_kernel,
        [((32, 6144), BF), ((32, 6144), BF), ((16, 128, 128), BF)]
        + [((72, 128), F32)] * 8,
        (glue, inputs, rcv, cotangent, halos, wb, wbt, lw, lwt, perm, edge, rev),
        1,
        [
            pltpu.VMEM((512, 512), BF), pltpu.VMEM((1024, 1024), BF), pltpu.VMEM((128, 1024), BF),
            pltpu.VMEM((256, 1024), F32), pltpu.VMEM((256, 1024), F32), pltpu.VMEM((256, 1024), BF),
            pltpu.VMEM((256, 1024), BF), pltpu.VMEM((576, 128), F32), pltpu.VMEM((64, 4096), BF),
            pltpu.VMEM((128, 1024), BF),
        ],
        name="main",
    )
    rims = plane(pay)
    rback = swap(back)
    w = total([hop(chunks[k], ("l", "c", "h"), 8, k) for k in range(8)])
    w = total([ring(w, "z", k) for k in range(4)])
    w = total([ring(w, "x", k) for k in range(4)])
    parts = [hop(w, ("l", "c"), 4, k) for k in range(4)]
    outgoing = call(
        route_rims_kernel,
        ((8, 128, 128), BF),
        (codes, rims),
        1,
        [pltpu.VMEM((1024, 128), F32)],
        name="route_rims",
    )
    ret = octet(outgoing)
    gin, lev = call(
        final_kernel,
        [((2, 32, 4096), BF), ((2, 64, 1024), BF)],
        (glue, ret, keep, rback, perm, edge, rev),
        1,
        [pltpu.VMEM((64, 4096), BF), pltpu.VMEM((512, 512), BF)],
        name="final",
    )
    gc, gl = call(
        unpack_kernel,
        [((9, 32, 64), F32), ((32, 2, 2, 128), F32)],
        tuple(parts),
        0,
        [pltpu.VMEM((288, 128), F32)],
        name="unpack",
    )
    grad_conv = jnp.transpose(gc.reshape(3, 3, 32, 64), (3, 2, 0, 1))
    grad_level = jnp.transpose(gl, (3, 0, 1, 2))
    return lev, gin, grad_conv, grad_level


def solution(mesh):
    fine = Mesh(mesh.devices.reshape(4, 4, 2, 2, 2), ("z", "x", "l", "c", "h"))
    tile = ("z", "x", "l", "c")
    return jax.shard_map(
        on_device,
        mesh=fine,
        in_specs=(
            P(tile, "h", None),
            P(tile, None, None),
            P(),
            P(),
            P(tile, "h", None),
        ),
        out_specs=(
            P(tile, "h", None),
            P(tile, "h", None),
            P(None, "h", None, None),
            P(None, "h", None, None),
        ),
        check_vma=False,
    )
```

```python
import jax
import jax.numpy as jnp
import numpy as np
from jax import lax
from jax.experimental import pallas as pl
from jax.experimental.pallas import tpu as pltpu
from jax.sharding import Mesh
from jax.sharding import PartitionSpec as P

BF = jnp.bfloat16
F32 = jnp.float32
NT = (((1,), (1,)), ((), ()))
SQ = float(np.sqrt(2.0 / np.pi))


def constants():
    perm = np.zeros((512, 512), np.float32)
    for i in range(8):
        for j in range(64):
            perm[i * 64 + j, ((i % 2) * 2 + j % 2) * 128 + (i // 2) * 32 + j // 2] = 1
    edge = np.zeros((128, 2048), np.float32)
    pick = np.zeros((4096, 128), np.float32)
    for side in range(2):
        for a in range(2):
            for x in range(32):
                k = side * 64 + a * 32 + x
                edge[k, a * 1024 + x * 32 + 31 * side] = 1
                pick[(2 * x + a) * 64 + 63 * side, k] = 1
    ends = np.zeros((256, 128), np.float32)
    for b in range(2):
        for y in range(32):
            ends[2 * y + b, b * 32 + y] = 1
            ends[128 + 64 + 2 * y + b, 64 + b * 32 + y] = 1
    rev = np.zeros((128, 128), np.float32)
    for half in range(2):
        for i in range(64):
            rev[half * 64 + i, half * 64 + 63 - i] = 1
    return [jnp.asarray(m, BF) for m in (perm, edge, pick, ends, rev)]


def dot(a, b):
    return jnp.dot(a, b, preferred_element_type=F32)


def dot_nt(a, b):
    return lax.dot_general(a, b, NT, preferred_element_type=F32)


def al(v, m):
    return pl.multiple_of(v, m)


def strips_kernel(glue, inp, cot, pick, ends, out, send):
    pix = inp[...].reshape(64, 4096)
    lr = dot(pix, pick[...]).astype(BF)
    tb = dot(jnp.concatenate([pix[:, :128], pix[:, 3968:]], axis=1), ends[...]).astype(BF)
    lane = lax.broadcasted_iota(jnp.int32, (16, 128), 1)
    codes = jnp.zeros((16, 128), jnp.int32)
    for tile in range(2):
        for side in range(4):
            t, s = glue[0, tile, side], glue[1, tile, side]
            k = tile * 4 + side
            codes = jnp.where(lane == k, t >> 3, codes)
            codes = jnp.where(lane == k + 8, (t & 7) * 4 + s, codes)
    codes = codes.astype(F32).astype(BF)
    for d in range(16):
        for tile in range(2):
            out[d, tile * 64 : tile * 64 + 32, :] = tb[tile * 32 : tile * 32 + 32]
            out[d, tile * 64 + 32 : tile * 64 + 64, :] = lr[tile * 32 : tile * 32 + 32]
        out[d, 128:144, :] = codes
    o = 1 - lax.axis_index("h")
    send[:, :4096] = inp[o]
    send[:, 4096:5120] = cot[o, :32]
    send[:, 5120:] = cot[o, 32:]


def weight_kernel(w, lwc, wb, wbt, lw, lwt):
    wb[...] = jnp.zeros((256, 1024), BF)
    for a in range(2):
        for b in range(2):
            ab = (a * 2 + b) * 64
            for i in range(3):
                for j in range(3):
                    rs = ((a + i) * 4 + b + j) * 64
                    wb[ab : ab + 64, rs : rs + 64] = w[i, j]
    wbt[...] = wb[...].T
    row = lax.broadcasted_iota(jnp.int32, (256, 256), 0)
    col = lax.broadcasted_iota(jnp.int32, (256, 256), 1)
    order = jnp.where((row & 63) * 4 + (row >> 6) == col, 1.0, 0.0).astype(BF)
    v = dot(order, lwc[...]).astype(BF)
    lwt[...] = v
    lw[...] = v.T


def place(acc, row, v, flip_half, dst_side, half):
    v = pltpu.roll(v, flip_half * 64, 1)
    acc[pl.ds(row, 32), :] = jnp.where(half == (dst_side & 1), v, acc[pl.ds(row, 32), :])


def route_strips_kernel(codes, got, out, acc):
    acc[...] = jnp.zeros((512, 128), F32)
    half = lax.broadcasted_iota(jnp.int32, (32, 128), 1) // 64

    @pl.loop(0, 16)
    def _(i):
        for m in range(8):
            c = codes[i * 8 + m]
            r = m & 3

            @pl.when(c >= 0)
            def _(m=m, c=c, r=r):
                v = got[i, (m >> 1) * 32 : (m >> 1) * 32 + 32, :].astype(F32)
                place(acc, al((c >> 1) * 32, 32), v, (r ^ c) & 1, c, half)

    for k in range(8):
        out[k] = acc[k * 64 : k * 64 + 64, :].astype(BF)


def flip(strips, rev, first, second):
    n = strips.shape[0]
    turned = dot(strips.astype(BF), rev)
    lane = lax.broadcasted_iota(jnp.int32, (n, 128), 1)
    flag = jnp.where(lane < 64, first, second)
    return jnp.where(flag == 1, turned, strips)


def main_kernel(
    glue, inp, rcv, cot, halo, wb, wbt, lw, lwt, perm, edge, rev,
    keep, send, pay, c0, c1, c2, c3, c4, c5, c6, c7,
    xs, pt, ct, pre_s, gh_s, hd, gp, wh, gs, lv_s,
):
    h = lax.axis_index("h")
    mine, other = h * 32, 32 - h * 32
    for g in range(8):
        xs[pl.ds(al(g * 64 + mine, 32), 32), :] = inp[h, :, g * 512 : g * 512 + 512]
        xs[pl.ds(al(g * 64 + other, 32), 32), :] = rcv[:, g * 512 : g * 512 + 512]
    ct[pl.ds(al(h * 64, 64), 64), :] = cot[h]
    ct[pl.ds(al(64 - h * 64, 64), 32), :] = rcv[:, 4096:5120]
    ct[pl.ds(al(96 - h * 64, 32), 32), :] = rcv[:, 5120:]
    nat = dot(xs[...], perm[...])
    ph = [
        [
            jnp.concatenate(
                [nat[g * 64 : g * 64 + 64, (a * 2 + b) * 128 : (a * 2 + b) * 128 + 128] for g in range(8)],
                axis=1,
            )
            for b in range(2)
        ]
        for a in range(2)
    ]
    parts = []
    for q in range(2):
        t = [halo[k].astype(F32) for k in range(q, 8, 2)]
        parts.append((t[0] + t[1]) + (t[2] + t[3]))
    tb, lr = (
        jnp.concatenate([parts[0][k : k + 32], parts[1][k : k + 32]], axis=0) for k in (0, 32)
    )
    fl = [glue[2, h, s] for s in range(4)]
    tb = flip(tb, rev[...], fl[0], fl[1])
    lr = flip(lr, rev[...], fl[2], fl[3])
    sp = dot(lr.astype(BF), edge[...])
    lane = lax.broadcasted_iota(jnp.int32, (64, 1024), 1)
    y = lane & 31
    l1 = lax.broadcasted_iota(jnp.int32, (64, 128), 1)
    cols = [[None] * 4 for _ in range(2)]
    for a in range(2):
        spa = sp[:, a * 1024 : a * 1024 + 1024]
        cols[a][0] = jnp.where(y == 0, spa, pltpu.roll(ph[a][1], 1, 1))
        cols[a][1] = ph[a][0]
        cols[a][2] = ph[a][1]
        cols[a][3] = jnp.where(y == 31, spa, pltpu.roll(ph[a][0], 1023, 1))
    top_shift = (97, 0, 96, 127)
    low_shift = (1, 32, 0, 31)
    for s in range(4):
        pt[(4 + s) * 64 : (4 + s) * 64 + 64, :] = cols[0][s].astype(BF)
        pt[(8 + s) * 64 : (8 + s) * 64 + 64, :] = cols[1][s].astype(BF)
        up = pltpu.roll(cols[1][s], 32, 1)
        t = pltpu.roll(tb, top_shift[s], 1) if top_shift[s] else tb
        if s == 0:
            t = jnp.where(l1 == 0, 0.0, t)
        if s == 3:
            t = jnp.where(l1 == 31, 0.0, t)
        pt[s * 64 : s * 64 + 64, 128:] = up[:, 128:].astype(BF)
        pt[s * 64 : s * 64 + 64, :128] = jnp.where(l1 < 32, t, up[:, :128]).astype(BF)
        dn = pltpu.roll(cols[0][s], 992, 1)
        t = pltpu.roll(tb, low_shift[s], 1) if low_shift[s] else tb
        if s == 0:
            t = jnp.where(l1 == 96, 0.0, t)
        if s == 3:
            t = jnp.where(l1 == 127, 0.0, t)
        pt[(12 + s) * 64 : (12 + s) * 64 + 64, :896] = dn[:, :896].astype(BF)
        pt[(12 + s) * 64 : (12 + s) * 64 + 64, 896:] = jnp.where(l1 >= 96, t, dn[:, 896:]).astype(BF)
    pre_s[...] = dot(wb[...], pt[...])
    gh_s[...] = dot(lwt[...], ct[...])
    for q in range(8):
        rows = slice(q * 32, q * 32 + 32)
        v = pre_s[rows, :]
        v2 = v * v
        half = 0.5 + 0.5 * jnp.tanh(v * (SQ + (SQ * 0.044715) * v2))
        act = v * half
        hd[rows, :] = act.astype(BF)
        d = half + act * (1.0 - half) * (2 * SQ + (6 * SQ * 0.044715) * v2)
        gp[rows, :] = (gh_s[rows, :] * d).astype(BF)
    gx = dot(wbt[...], gp[...])

    def blk(r, s):
        k = (r * 4 + s) * 64
        return gx[k : k + 64]

    x0 = lane < 32
    x31 = lane >= 992

    def down(v):
        return jnp.where(x0, 0.0, pltpu.roll(v, 32, 1))

    def up_(v):
        return jnp.where(x31, 0.0, pltpu.roll(v, 992, 1))

    qs, ms = [], []
    for r in range(4):
        q0 = blk(r, 1) + jnp.where(y == 0, 0.0, pltpu.roll(blk(r, 3), 1, 1))
        q1 = blk(r, 2) + jnp.where(y == 31, 0.0, pltpu.roll(blk(r, 0), 1023, 1))
        qs.append((q0, q1))
        ms.append(jnp.where(y == 0, blk(r, 0), jnp.where(y == 31, blk(r, 3), 0.0)))
    top = jnp.where(l1 < 32, qs[0][0][:, :128], pltpu.roll(qs[0][1][:, :128], 32, 1))
    low = jnp.where(l1 < 96, pltpu.roll(qs[3][0][:, 896:], 96, 1), qs[3][1][:, 896:])
    rim_tb = jnp.where(l1 < 64, top, low).astype(BF)
    a0 = (ms[1] + down(ms[3])).astype(BF)
    a1 = (ms[2] + up_(ms[0])).astype(BF)
    rim_lr = dot_nt(a0, edge[:, :1024]) + dot_nt(a1, edge[:, 1024:])
    rim_lr = rim_lr.astype(BF)
    for d in range(16):
        pay[d, 0:64, :] = rim_tb
        pay[d, 64:128, :] = rim_lr
    dl = dot_nt(hd[...], ct[...])
    gbt = dot_nt(pt[...], gp[...])
    packed = []
    for ij in range(9):
        i, j = divmod(ij, 3)
        u = v = None
        for a in range(2):
            k = ((a + i) * 4 + j) * 64
            ua = gbt[k : k + 64, a * 128 : a * 128 + 128]
            va = gbt[k + 64 : k + 128, a * 128 : a * 128 + 128]
            u = ua if u is None else u + ua
            v = va if v is None else v + va
        if ij % 2 == 0:
            packed.append(jnp.where(l1 < 64, u + pltpu.roll(v, 64, 1), 0.0))
        else:
            packed[-1] = jnp.where(l1 < 64, packed[-1], v + pltpu.roll(u, 64, 1))
    for hh in range(2):
        base = hh * 288
        for q in range(5):
            wh[base + q * 32 : base + q * 32 + 32, :] = packed[q][hh * 32 : hh * 32 + 32]
        for ab in range(4):
            row = base + 160 + ab * 32
            wh[row : row + 32, :] = dl[ab * 64 + hh * 32 : ab * 64 + hh * 32 + 32]
    lch = lax.axis_index("l") * 4 + lax.axis_index("c") * 2 + h
    for k, ref in enumerate((c0, c1, c2, c3, c4, c5, c6, c7)):
        d = lch ^ k
        ref[...] = wh[pl.ds(al((d & 1) * 288 + (d >> 1) * 72, 8), 72), :]
    lv_s[...] = dot(lw[...], hd[...]).astype(BF)
    for b in range(2):
        gs[:, b * 1024 : b * 1024 + 1024] = (qs[1][b] + down(qs[3][b])).astype(BF)
        gs[:, 2048 + b * 1024 : 3072 + b * 1024] = (qs[2][b] + up_(qs[0][b])).astype(BF)
    for ref, row in ((keep, h * 32), (send, 32 - h * 32)):
        ref[:, :4096] = gs[pl.ds(al(row, 32), 32), :]
        ref[:, 4096:5120] = lv_s[pl.ds(al(row * 2, 64), 32), :]
        ref[:, 5120:] = lv_s[pl.ds(al(row * 2 + 32, 32), 32), :]


def route_rims_kernel(codes, got, out, acc):
    acc[...] = jnp.zeros((1024, 128), F32)
    half = lax.broadcasted_iota(jnp.int32, (32, 128), 1) // 64
    h = lax.axis_index("h")

    @pl.loop(0, 16)
    def _(i):
        for r in range(4):
            c = codes[i * 8 + h * 4 + r]

            @pl.when(c >= 0)
            def _(c=c, r=r):
                t, s = c >> 2, c & 3
                for hh in range(2):
                    row = (r >> 1) * 64 + hh * 32
                    v = got[i, row : row + 32, :].astype(F32)
                    dst = ((t & 6) | hh) * 128 + (t & 1) * 64 + (s >> 1) * 32
                    place(acc, al(dst, 32), v, (r ^ s) & 1, s, half)

    for k in range(8):
        out[k] = acc[k * 128 : k * 128 + 128, :].astype(BF)


def final_kernel(glue, ret, keep, rcv, perm, edge, rev, gin, lev, gs, xs):
    h = lax.axis_index("h")
    acc = ret[0].astype(F32)
    for k in range(1, 8):
        acc = acc + ret[k].astype(F32)
    lane = lax.broadcasted_iota(jnp.int32, (128, 128), 1)
    row = lax.broadcasted_iota(jnp.int32, (128, 128), 0)
    flag = jnp.zeros((128, 128), jnp.int32)
    for tile in range(2):
        for side in range(4):
            here = ((row >> 5) == tile * 2 + (side >> 1)) & ((lane >> 6) == (side & 1))
            flag = jnp.where(here, glue[2, tile, side], flag)
    turned = dot(acc.astype(BF), rev[...])
    acc = jnp.where(flag == 1, turned, acc)
    tb = jnp.concatenate([acc[0:32], acc[64:96]], axis=0)
    lr = jnp.concatenate([acc[32:64], acc[96:128]], axis=0)
    sp = dot(lr.astype(BF), edge[...])
    gs[pl.ds(al(h * 32, 32), 32), :] = keep[:, :4096]
    gs[pl.ds(al(32 - h * 32, 32), 32), :] = rcv[:, :4096]
    y = lax.broadcasted_iota(jnp.int32, (64, 1024), 1) & 31
    l1 = lax.broadcasted_iota(jnp.int32, (64, 128), 1)
    for a in range(2):
        for b in range(2):
            ab = a * 2 + b
            v = gs[:, ab * 1024 : ab * 1024 + 1024].astype(F32)
            v = v + jnp.where(y == 31 * b, sp[:, a * 1024 : a * 1024 + 1024], 0.0)
            shift = ((0, 96), (32, 0))[a][b]
            t = pltpu.roll(tb, shift, 1) if shift else tb
            t = jnp.where((l1 >= 96) if a else (l1 < 32), t, 0.0)
            for g in range(8):
                part = v[:, g * 128 : g * 128 + 128]
                if g == 7 * a:
                    part = part + t
                xs[g * 64 : g * 64 + 64, ab * 128 : ab * 128 + 128] = part.astype(BF)
    nat = dot_nt(xs[...], perm[...]).astype(BF)
    for g in range(8):
        for tile in range(2):
            k = g * 64 + tile * 32
            gin[tile, :, g * 512 : g * 512 + 512] = nat[k : k + 32]
    for tile, src in ((h, keep), (1 - h, rcv)):
        lev[tile, :32] = src[:, 4096:5120]
        lev[tile, 32:] = src[:, 5120:]


def unpack_kernel(w0, w1, w2, w3, gc, gl, w):
    q = lax.axis_index("l") * 2 + lax.axis_index("c")
    for k, ref in enumerate((w0, w1, w2, w3)):
        w[pl.ds(al((q ^ k) * 72, 8), 72), :] = ref[...]
    for ij in range(9):
        v = w[(ij // 2) * 32 : (ij // 2) * 32 + 32, :]
        if ij % 2:
            v = pltpu.roll(v, 64, 1)
        gc[ij] = v[:, :64]
    for ab in range(4):
        gl[:, ab // 2, ab % 2, :] = w[160 + ab * 32 : 192 + ab * 32, :]


def call(kernel, outs, args, smem, scratch=(), mib=8):
    specs = [
        pl.BlockSpec(memory_space=pltpu.SMEM if i < smem else pltpu.VMEM) for i in range(len(args))
    ]
    single = not isinstance(outs, list)
    shapes = [outs] if single else outs
    res = pl.pallas_call(
        kernel,
        out_shape=[jax.ShapeDtypeStruct(s, d) for s, d in shapes],
        in_specs=specs,
        out_specs=[pl.BlockSpec(memory_space=pltpu.VMEM) for _ in shapes],
        scratch_shapes=list(scratch),
        compiler_params=pltpu.CompilerParams(vmem_limit_bytes=mib << 20),
    )(*args)
    return res[0] if single else res


def swap(v):
    return lax.ppermute(v, "h", [(0, 1), (1, 0)])


def hop(v, axes, n, k):
    return lax.ppermute(v, axes, [(i, i ^ k) for i in range(n)]) if k else v


def ring(v, axis, k):
    return lax.ppermute(v, axis, [(i, (i + k) % 4) for i in range(4)]) if k else v


def total(parts):
    while len(parts) > 1:
        parts = [a + b for a, b in zip(parts[::2], parts[1::2])]
    return parts[0]


def plane(v):
    return lax.all_to_all(v, ("z", "x"), 0, 0)


def octet(v):
    return lax.all_to_all(v, ("l", "c", "h"), 0, 0)


def level_step(inputs, gluing, conv_weight, level_weight, cotangent):
    perm, edge, pick, ends, rev = constants()
    glue = jnp.transpose(gluing, (2, 0, 1))
    strips, send = call(
        strips_kernel,
        [((16, 144, 128), BF), ((32, 6144), BF)],
        (glue, inputs, cotangent, pick, ends),
        1,
        mib=58,
    )
    rcv = swap(send)
    got = plane(strips)
    here = (lax.axis_index("z") * 4 + lax.axis_index("x")).astype(BF)
    codes = jnp.where(got[:, 128, :8] == here, got[:, 128, 8:16], -1).astype(jnp.int32).reshape(128)
    routed = call(
        route_strips_kernel, ((8, 64, 128), BF), (codes, got), 1, [pltpu.VMEM((512, 128), F32)]
    )
    halos = octet(routed)
    w9 = jnp.transpose(conv_weight, (2, 3, 0, 1))
    lwc = jnp.transpose(level_weight, (1, 2, 3, 0)).reshape(256, 128)
    wb, wbt, lw, lwt = call(
        weight_kernel,
        [((256, 1024), BF), ((1024, 256), BF), ((128, 256), BF), ((256, 128), BF)],
        (w9, lwc),
        0,
        mib=58,
    )
    keep, back, pay, *chunks = call(
        main_kernel,
        [((32, 6144), BF), ((32, 6144), BF), ((16, 128, 128), BF)]
        + [((72, 128), F32)] * 8,
        (glue, inputs, rcv, cotangent, halos, wb, wbt, lw, lwt, perm, edge, rev),
        1,
        [
            pltpu.VMEM((512, 512), BF), pltpu.VMEM((1024, 1024), BF), pltpu.VMEM((128, 1024), BF),
            pltpu.VMEM((256, 1024), F32), pltpu.VMEM((256, 1024), F32), pltpu.VMEM((256, 1024), BF),
            pltpu.VMEM((256, 1024), BF), pltpu.VMEM((576, 128), F32), pltpu.VMEM((64, 4096), BF),
            pltpu.VMEM((128, 1024), BF),
        ],
        mib=58,
    )
    rims = plane(pay)
    rback = swap(back)
    near = [hop(chunks[k], ("l", "c", "h"), 8, k) for k in range(8)]
    w = total(near)
    near = [ring(w, "z", k) for k in range(4)]
    w = total(near)
    near = [ring(w, "x", k) for k in range(4)]
    w = total(near)
    parts = [hop(w, ("l", "c"), 4, k) for k in range(4)]
    outgoing = call(
        route_rims_kernel, ((8, 128, 128), BF), (codes, rims), 1, [pltpu.VMEM((1024, 128), F32)]
    )
    ret = octet(outgoing)
    gin, lev = call(
        final_kernel,
        [((2, 32, 4096), BF), ((2, 64, 1024), BF)],
        (glue, ret, keep, rback, perm, edge, rev),
        1,
        [pltpu.VMEM((64, 4096), BF), pltpu.VMEM((512, 512), BF)],
    )
    gc, gl = call(
        unpack_kernel,
        [((9, 32, 64), F32), ((32, 2, 2, 128), F32)],
        tuple(parts),
        0,
        [pltpu.VMEM((288, 128), F32)],
    )
    grad_conv = jnp.transpose(gc.reshape(3, 3, 32, 64), (3, 2, 0, 1))
    grad_level = jnp.transpose(gl, (3, 0, 1, 2))
    return lev, gin, grad_conv, grad_level


def solution(mesh):
    fine = Mesh(mesh.devices.reshape(4, 4, 2, 2, 2), ("z", "x", "l", "c", "h"))
    tile = ("z", "x", "l", "c")
    return jax.shard_map(
        level_step,
        mesh=fine,
        in_specs=(
            P(tile, "h", None),
            P(tile, None, None),
            P(),
            P(),
            P(tile, "h", None),
        ),
        out_specs=(
            P(tile, "h", None),
            P(tile, "h", None),
            P(None, "h", None, None),
            P(None, "h", None, None),
        ),
        check_vma=False,
    )
```

```python
import jax
import jax.numpy as jnp
import numpy as np
from jax import lax
from jax.experimental import pallas as pl
from jax.experimental.pallas import tpu as pltpu
from jax.sharding import Mesh
from jax.sharding import PartitionSpec as P

BF = jnp.bfloat16
F32 = jnp.float32
NT = (((1,), (1,)), ((), ()))
SQ = float(np.sqrt(2.0 / np.pi))


def constants():
    perm = np.zeros((512, 512), np.float32)
    for i in range(8):
        for j in range(64):
            perm[i * 64 + j, ((i % 2) * 2 + j % 2) * 128 + (i // 2) * 32 + j // 2] = 1
    edge = np.zeros((128, 2048), np.float32)
    for side in range(2):
        for a in range(2):
            for x in range(32):
                k = side * 64 + a * 32 + x
                edge[k, a * 1024 + x * 32 + 31 * side] = 1
    rev = np.zeros((128, 128), np.float32)
    for half in range(2):
        for i in range(64):
            rev[half * 64 + i, half * 64 + 63 - i] = 1
    return [jnp.asarray(m, BF) for m in (perm, edge, rev)]


def dot(a, b):
    return jnp.dot(a, b, preferred_element_type=F32)


def dot_nt(a, b):
    return lax.dot_general(a, b, NT, preferred_element_type=F32)


def al(v, m):
    return pl.multiple_of(v, m)


def select(rows, target):
    row = lax.broadcasted_iota(jnp.int32, (rows, target.shape[1]), 0)
    return jnp.where(row == target, 1.0, 0.0).astype(BF)


def columns(n):
    return lax.broadcasted_iota(jnp.int32, (1, n), 1)


def pick_matrix():
    k = columns(128)
    return select(512, (2 * (k & 31) + ((k >> 5) & 1)) * 64 + 63 * (k >> 6))


def ends_matrix():
    k = columns(128)
    return select(256, 2 * (k & 31) + ((k >> 5) & 1) + 192 * (k >> 6))


def collect(v):
    out = v[:64]
    for g in range(1, 8):
        out = out + pltpu.roll(v[g * 64 : g * 64 + 64], 4 * g, 1)
    return out


def strips_kernel(glue, inp, cot, out, send):
    pix = inp[...].reshape(64, 4096)
    stack = jnp.concatenate([pix[:, g * 512 : g * 512 + 512] for g in range(8)], axis=0)
    lr = collect(dot(stack, pick_matrix())).astype(BF)
    tb = dot(jnp.concatenate([pix[:, :128], pix[:, 3968:]], axis=1), ends_matrix()).astype(BF)
    lane = lax.broadcasted_iota(jnp.int32, (16, 128), 1)
    codes = jnp.zeros((16, 128), jnp.int32)
    for tile in range(2):
        for side in range(4):
            t, s = glue[0, tile, side], glue[1, tile, side]
            k = tile * 4 + side
            codes = jnp.where(lane == k, t >> 3, codes)
            codes = jnp.where(lane == k + 8, (t & 7) * 4 + s, codes)
    codes = codes.astype(F32).astype(BF)
    for d in range(16):
        for tile in range(2):
            out[d, tile * 64 : tile * 64 + 32, :] = tb[tile * 32 : tile * 32 + 32]
            out[d, tile * 64 + 32 : tile * 64 + 64, :] = lr[tile * 32 : tile * 32 + 32]
        out[d, 128:144, :] = codes
    o = 1 - lax.axis_index("h")
    send[:, :4096] = inp[o]
    send[:, 4096:5120] = cot[o, :32]
    send[:, 5120:] = cot[o, 32:]


def prepare_kernel(
    w, lwc, inp, rcv, cot, perm, edge, rev,
    wb, wbt, lw, lwt, ph, ct, edge_out, rev_out,
    w_v, lwc_v, inp_v, rcv_v, perm_v, xs, sems,
):
    h = lax.axis_index("h")
    mine, other = h * 32, 32 - h * 32
    copies = [
        pltpu.make_async_copy(src, dst, sems.at[k])
        for k, (src, dst) in enumerate(
            (
                (w, w_v), (lwc, lwc_v), (inp.at[h], inp_v), (rcv, rcv_v), (perm, perm_v),
                (cot.at[h], ct.at[pl.ds(al(h * 64, 64), 64), :]), (edge, edge_out), (rev, rev_out),
            )
        )
    ]
    for c in copies:
        c.start()
    wb[...] = jnp.zeros((256, 1024), BF)
    copies[0].wait()
    for a in range(2):
        for b in range(2):
            ab = (a * 2 + b) * 64
            for i in range(3):
                for j in range(3):
                    rs = ((a + i) * 4 + b + j) * 64
                    wb[ab : ab + 64, rs : rs + 64] = w_v[i, j]
    wbt[...] = wb[...].T
    row = lax.broadcasted_iota(jnp.int32, (256, 256), 0)
    col = lax.broadcasted_iota(jnp.int32, (256, 256), 1)
    order = jnp.where((row & 63) * 4 + (row >> 6) == col, 1.0, 0.0).astype(BF)
    copies[1].wait()
    v = dot(order, lwc_v[...]).astype(BF)
    lwt[...] = v
    lw[...] = v.T
    copies[2].wait()
    copies[3].wait()
    for g in range(8):
        xs[pl.ds(al(g * 64 + mine, 32), 32), :] = inp_v[:, g * 512 : g * 512 + 512]
        xs[pl.ds(al(g * 64 + other, 32), 32), :] = rcv_v[:, g * 512 : g * 512 + 512]
    ct[pl.ds(al(64 - h * 64, 64), 32), :] = rcv_v[:, 4096:5120]
    ct[pl.ds(al(96 - h * 64, 32), 32), :] = rcv_v[:, 5120:]
    copies[4].wait()
    nat = dot(xs[...], perm_v[...]).astype(BF)
    for ab in range(4):
        for g in range(8):
            ph[ab, :, g * 128 : g * 128 + 128] = nat[g * 64 : g * 64 + 64, ab * 128 : ab * 128 + 128]
    for c in copies[5:]:
        c.wait()


def place(acc, row, v, flip_half, dst_side, half):
    v = pltpu.roll(v, flip_half * 64, 1)
    acc[pl.ds(row, 32), :] = jnp.where(half == (dst_side & 1), v, acc[pl.ds(row, 32), :])


def route_strips_kernel(codes, got, out, acc):
    acc[...] = jnp.zeros((512, 128), F32)
    half = lax.broadcasted_iota(jnp.int32, (32, 128), 1) // 64

    @pl.loop(0, 16, unroll=4)
    def _(i):
        for m in range(8):
            c = codes[i * 8 + m]
            r = m & 3

            @pl.when(c >= 0)
            def _(m=m, c=c, r=r):
                v = got[i, (m >> 1) * 32 : (m >> 1) * 32 + 32, :].astype(F32)
                place(acc, al((c >> 1) * 32, 32), v, (r ^ c) & 1, c, half)

    for k in range(8):
        out[k] = acc[k * 64 : k * 64 + 64, :].astype(BF)


def flip(strips, rev, first, second):
    n = strips.shape[0]
    turned = dot(strips.astype(BF), rev)
    lane = lax.broadcasted_iota(jnp.int32, (n, 128), 1)
    flag = jnp.where(lane < 64, first, second)
    return jnp.where(flag == 1, turned, strips)


def main_kernel(
    glue, halo, wb, wbt, lw, lwt, phs, ct, edge, rev,
    keep, send, pay, c0, c1, c2, c3, c4, c5, c6, c7,
    pt, pre_s, gh_s, hd, gp, wh, gs, lv_s, rim, sems,
):
    h = lax.axis_index("h")
    ph = [[phs[a * 2 + b].astype(F32) for b in range(2)] for a in range(2)]
    parts = []
    for q in range(2):
        t = [halo[k].astype(F32) for k in range(q, 8, 2)]
        parts.append((t[0] + t[1]) + (t[2] + t[3]))
    tb, lr = (
        jnp.concatenate([parts[0][k : k + 32], parts[1][k : k + 32]], axis=0) for k in (0, 32)
    )
    fl = [glue[2, h, s] for s in range(4)]
    tb = flip(tb, rev[...], fl[0], fl[1])
    lr = flip(lr, rev[...], fl[2], fl[3])
    sp = dot(lr.astype(BF), edge[...])
    lane = lax.broadcasted_iota(jnp.int32, (64, 1024), 1)
    y = lane & 31
    l1 = lax.broadcasted_iota(jnp.int32, (64, 128), 1)
    cols = [[None] * 4 for _ in range(2)]
    for a in range(2):
        spa = sp[:, a * 1024 : a * 1024 + 1024]
        cols[a][0] = jnp.where(y == 0, spa, pltpu.roll(ph[a][1], 1, 1))
        cols[a][1] = ph[a][0]
        cols[a][2] = ph[a][1]
        cols[a][3] = jnp.where(y == 31, spa, pltpu.roll(ph[a][0], 1023, 1))
    top_shift = (97, 0, 96, 127)
    low_shift = (1, 32, 0, 31)
    for s in range(4):
        pt[(4 + s) * 64 : (4 + s) * 64 + 64, :] = cols[0][s].astype(BF)
        pt[(8 + s) * 64 : (8 + s) * 64 + 64, :] = cols[1][s].astype(BF)
        up = pltpu.roll(cols[1][s], 32, 1)
        t = pltpu.roll(tb, top_shift[s], 1) if top_shift[s] else tb
        if s == 0:
            t = jnp.where(l1 == 0, 0.0, t)
        if s == 3:
            t = jnp.where(l1 == 31, 0.0, t)
        pt[s * 64 : s * 64 + 64, 128:] = up[:, 128:].astype(BF)
        pt[s * 64 : s * 64 + 64, :128] = jnp.where(l1 < 32, t, up[:, :128]).astype(BF)
        dn = pltpu.roll(cols[0][s], 992, 1)
        t = pltpu.roll(tb, low_shift[s], 1) if low_shift[s] else tb
        if s == 0:
            t = jnp.where(l1 == 96, 0.0, t)
        if s == 3:
            t = jnp.where(l1 == 127, 0.0, t)
        pt[(12 + s) * 64 : (12 + s) * 64 + 64, :896] = dn[:, :896].astype(BF)
        pt[(12 + s) * 64 : (12 + s) * 64 + 64, 896:] = jnp.where(l1 >= 96, t, dn[:, 896:]).astype(BF)
    pre_s[...] = dot(wb[...], pt[...])
    gh_s[...] = dot(lwt[...], ct[...])
    for q in range(8):
        rows = slice(q * 32, q * 32 + 32)
        v = pre_s[rows, :]
        v2 = v * v
        half = 0.5 + 0.5 * jnp.tanh(v * (SQ + (SQ * 0.044715) * v2))
        act = v * half
        hd[rows, :] = act.astype(BF)
        d = half + act * (1.0 - half) * (2 * SQ + (6 * SQ * 0.044715) * v2)
        gp[rows, :] = (gh_s[rows, :] * d).astype(BF)
    gx = dot(wbt[...], gp[...])

    def blk(r, s):
        k = (r * 4 + s) * 64
        return gx[k : k + 64]

    x0 = lane < 32
    x31 = lane >= 992

    def down(v):
        return jnp.where(x0, 0.0, pltpu.roll(v, 32, 1))

    def up_(v):
        return jnp.where(x31, 0.0, pltpu.roll(v, 992, 1))

    qs, ms = [], []
    for r in range(4):
        q0 = blk(r, 1) + jnp.where(y == 0, 0.0, pltpu.roll(blk(r, 3), 1, 1))
        q1 = blk(r, 2) + jnp.where(y == 31, 0.0, pltpu.roll(blk(r, 0), 1023, 1))
        qs.append((q0, q1))
        ms.append(jnp.where(y == 0, blk(r, 0), jnp.where(y == 31, blk(r, 3), 0.0)))
    top = jnp.where(l1 < 32, qs[0][0][:, :128], pltpu.roll(qs[0][1][:, :128], 32, 1))
    low = jnp.where(l1 < 96, pltpu.roll(qs[3][0][:, 896:], 96, 1), qs[3][1][:, 896:])
    rim_tb = jnp.where(l1 < 64, top, low).astype(BF)
    a0 = (ms[1] + down(ms[3])).astype(BF)
    a1 = (ms[2] + up_(ms[0])).astype(BF)
    rim_lr = dot_nt(a0, edge[:, :1024]) + dot_nt(a1, edge[:, 1024:])
    rim_lr = rim_lr.astype(BF)
    rim[0:64, :] = rim_tb
    rim[64:128, :] = rim_lr
    copies = [pltpu.make_async_copy(rim, pay.at[d], sems.at[d]) for d in range(16)]
    for c in copies:
        c.start()
    dl = dot_nt(hd[...], ct[...])
    gbt = dot_nt(pt[...], gp[...])
    packed = []
    for ij in range(9):
        i, j = divmod(ij, 3)
        u = v = None
        for a in range(2):
            k = ((a + i) * 4 + j) * 64
            ua = gbt[k : k + 64, a * 128 : a * 128 + 128]
            va = gbt[k + 64 : k + 128, a * 128 : a * 128 + 128]
            u = ua if u is None else u + ua
            v = va if v is None else v + va
        if ij % 2 == 0:
            packed.append(jnp.where(l1 < 64, u + pltpu.roll(v, 64, 1), 0.0))
        else:
            packed[-1] = jnp.where(l1 < 64, packed[-1], v + pltpu.roll(u, 64, 1))
    for hh in range(2):
        base = hh * 288
        for q in range(5):
            wh[base + q * 32 : base + q * 32 + 32, :] = packed[q][hh * 32 : hh * 32 + 32]
        for ab in range(4):
            row = base + 160 + ab * 32
            wh[row : row + 32, :] = dl[ab * 64 + hh * 32 : ab * 64 + hh * 32 + 32]
    lch = lax.axis_index("l") * 4 + lax.axis_index("c") * 2 + h
    for k, ref in enumerate((c0, c1, c2, c3, c4, c5, c6, c7)):
        d = lch ^ k
        row = al((d & 1) * 288 + (d >> 1) * 72, 8)
        copies.append(pltpu.make_async_copy(wh.at[pl.ds(row, 72), :], ref, sems.at[16 + k]))
        copies[-1].start()
    lv_s[...] = dot(lw[...], hd[...]).astype(BF)
    for b in range(2):
        gs[:, b * 1024 : b * 1024 + 1024] = (qs[1][b] + down(qs[3][b])).astype(BF)
        gs[:, 2048 + b * 1024 : 3072 + b * 1024] = (qs[2][b] + up_(qs[0][b])).astype(BF)
    n = 24
    for ref, row in ((send, 32 - h * 32), (keep, h * 32)):
        for src, first, dst in (
            (gs, al(row, 32), slice(0, 4096)),
            (lv_s, al(row * 2, 64), slice(4096, 5120)),
            (lv_s, al(row * 2 + 32, 32), slice(5120, 6144)),
        ):
            copies.append(
                pltpu.make_async_copy(src.at[pl.ds(first, 32), :], ref.at[:, dst], sems.at[n])
            )
            copies[-1].start()
            n += 1
    for c in copies:
        c.wait()


def route_rims_kernel(codes, got, out, acc):
    acc[...] = jnp.zeros((1024, 128), F32)
    half = lax.broadcasted_iota(jnp.int32, (32, 128), 1) // 64
    h = lax.axis_index("h")

    @pl.loop(0, 16, unroll=4)
    def _(i):
        for r in range(4):
            c = codes[i * 8 + h * 4 + r]

            @pl.when(c >= 0)
            def _(c=c, r=r):
                t, s = c >> 2, c & 3
                for hh in range(2):
                    row = (r >> 1) * 64 + hh * 32
                    v = got[i, row : row + 32, :].astype(F32)
                    dst = ((t & 6) | hh) * 128 + (t & 1) * 64 + (s >> 1) * 32
                    place(acc, al(dst, 32), v, (r ^ s) & 1, s, half)

    for k in range(8):
        out[k] = acc[k * 128 : k * 128 + 128, :].astype(BF)


def final_kernel(glue, ret, keep, rcv, perm, edge, rev, gin, lev, gs, xs):
    h = lax.axis_index("h")
    acc = ret[0].astype(F32)
    for k in range(1, 8):
        acc = acc + ret[k].astype(F32)
    lane = lax.broadcasted_iota(jnp.int32, (128, 128), 1)
    row = lax.broadcasted_iota(jnp.int32, (128, 128), 0)
    flag = jnp.zeros((128, 128), jnp.int32)
    for tile in range(2):
        for side in range(4):
            here = ((row >> 5) == tile * 2 + (side >> 1)) & ((lane >> 6) == (side & 1))
            flag = jnp.where(here, glue[2, tile, side], flag)
    turned = dot(acc.astype(BF), rev[...])
    acc = jnp.where(flag == 1, turned, acc)
    tb = jnp.concatenate([acc[0:32], acc[64:96]], axis=0)
    lr = jnp.concatenate([acc[32:64], acc[96:128]], axis=0)
    sp = dot(lr.astype(BF), edge[...])
    gs[pl.ds(al(h * 32, 32), 32), :] = keep[:, :4096]
    gs[pl.ds(al(32 - h * 32, 32), 32), :] = rcv[:, :4096]
    y = lax.broadcasted_iota(jnp.int32, (64, 1024), 1) & 31
    l1 = lax.broadcasted_iota(jnp.int32, (64, 128), 1)
    for a in range(2):
        for b in range(2):
            ab = a * 2 + b
            v = gs[:, ab * 1024 : ab * 1024 + 1024].astype(F32)
            v = v + jnp.where(y == 31 * b, sp[:, a * 1024 : a * 1024 + 1024], 0.0)
            shift = ((0, 96), (32, 0))[a][b]
            t = pltpu.roll(tb, shift, 1) if shift else tb
            t = jnp.where((l1 >= 96) if a else (l1 < 32), t, 0.0)
            for g in range(8):
                part = v[:, g * 128 : g * 128 + 128]
                if g == 7 * a:
                    part = part + t
                xs[g * 64 : g * 64 + 64, ab * 128 : ab * 128 + 128] = part.astype(BF)
    nat = dot_nt(xs[...], perm[...]).astype(BF)
    for g in range(8):
        for tile in range(2):
            k = g * 64 + tile * 32
            gin[tile, :, g * 512 : g * 512 + 512] = nat[k : k + 32]
    for tile, src in ((h, keep), (1 - h, rcv)):
        lev[tile, :32] = src[:, 4096:5120]
        lev[tile, 32:] = src[:, 5120:]


def unpack_kernel(w0, w1, w2, w3, gc, gl, w):
    q = lax.axis_index("l") * 2 + lax.axis_index("c")
    for k, ref in enumerate((w0, w1, w2, w3)):
        w[pl.ds(al((q ^ k) * 72, 8), 72), :] = ref[...]
    for ij in range(9):
        v = w[(ij // 2) * 32 : (ij // 2) * 32 + 32, :]
        if ij % 2:
            v = pltpu.roll(v, 64, 1)
        gc[ij] = v[:, :64]
    for ab in range(4):
        gl[:, ab // 2, ab % 2, :] = w[160 + ab * 32 : 192 + ab * 32, :]


def call(kernel, outs, args, smem, scratch=(), mib=8, far_in=False, far_out=False):
    near = pl.BlockSpec(memory_space=pltpu.VMEM)
    far = pl.BlockSpec(memory_space=pltpu.HBM)
    specs = [
        pl.BlockSpec(memory_space=pltpu.SMEM) if i < smem else far if far_in else near
        for i in range(len(args))
    ]
    single = not isinstance(outs, list)
    shapes = [outs] if single else outs
    res = pl.pallas_call(
        kernel,
        out_shape=[jax.ShapeDtypeStruct(s, d) for s, d in shapes],
        in_specs=specs,
        out_specs=[far if far_out else near for _ in shapes],
        scratch_shapes=list(scratch),
        compiler_params=pltpu.CompilerParams(vmem_limit_bytes=mib << 20),
    )(*args)
    return res[0] if single else res


def swap(v):
    return lax.ppermute(v, "h", [(0, 1), (1, 0)])


def hop(v, axes, n, k):
    return lax.ppermute(v, axes, [(i, i ^ k) for i in range(n)]) if k else v


def ring(v, axis, k):
    return lax.ppermute(v, axis, [(i, (i + k) % 4) for i in range(4)]) if k else v


def total(parts):
    while len(parts) > 1:
        parts = [a + b for a, b in zip(parts[::2], parts[1::2])]
    return parts[0]


def plane(v):
    return lax.all_to_all(v, ("z", "x"), 0, 0)


def octet(v):
    return lax.all_to_all(v, ("l", "c", "h"), 0, 0)


def level_step(inputs, gluing, conv_weight, level_weight, cotangent):
    perm, edge, rev = constants()
    glue = jnp.transpose(gluing, (2, 0, 1))
    strips, send = call(
        strips_kernel,
        [((16, 144, 128), BF), ((32, 6144), BF)],
        (glue, inputs, cotangent),
        1,
        mib=58,
    )
    rcv = swap(send)
    got = plane(strips)
    here = (lax.axis_index("z") * 4 + lax.axis_index("x")).astype(BF)
    codes = jnp.where(got[:, 128, :8] == here, got[:, 128, 8:16], -1).astype(jnp.int32).reshape(128)
    routed = call(
        route_strips_kernel, ((8, 64, 128), BF), (codes, got), 1, [pltpu.VMEM((512, 128), F32)]
    )
    halos = octet(routed)
    w9 = jnp.transpose(conv_weight, (2, 3, 0, 1))
    lwc = jnp.transpose(level_weight, (1, 2, 3, 0)).reshape(256, 128)
    wb, wbt, lw, lwt, ph, ct, edge_v, rev_v = call(
        prepare_kernel,
        [
            ((256, 1024), BF), ((1024, 256), BF), ((128, 256), BF), ((256, 128), BF),
            ((4, 64, 1024), BF), ((128, 1024), BF), ((128, 2048), BF), ((128, 128), BF),
        ],
        (w9, lwc, inputs, rcv, cotangent, perm, edge, rev),
        0,
        [
            pltpu.VMEM((3, 3, 64, 64), BF), pltpu.VMEM((256, 128), BF), pltpu.VMEM((32, 4096), BF),
            pltpu.VMEM((32, 6144), BF), pltpu.VMEM((512, 512), BF), pltpu.VMEM((512, 512), BF),
            pltpu.SemaphoreType.DMA((8,)),
        ],
        mib=58,
        far_in=True,
    )
    keep, back, pay, *chunks = call(
        main_kernel,
        [((32, 6144), BF), ((32, 6144), BF), ((16, 128, 128), BF)]
        + [((72, 128), F32)] * 8,
        (glue, halos, wb, wbt, lw, lwt, ph, ct, edge_v, rev_v),
        1,
        [
            pltpu.VMEM((1024, 1024), BF), pltpu.VMEM((256, 1024), F32), pltpu.VMEM((256, 1024), F32),
            pltpu.VMEM((256, 1024), BF), pltpu.VMEM((256, 1024), BF), pltpu.VMEM((576, 128), F32),
            pltpu.VMEM((64, 4096), BF), pltpu.VMEM((128, 1024), BF), pltpu.VMEM((128, 128), BF),
            pltpu.SemaphoreType.DMA((30,)),
        ],
        mib=58,
        far_out=True,
    )
    rims = plane(pay)
    rback = swap(back)
    near = [hop(chunks[k], ("l", "c", "h"), 8, k) for k in range(8)]
    w = total(near)
    near = [ring(w, "x", k) for k in range(4)]
    w = total(near)
    near = [ring(w, "z", k) for k in range(4)]
    w = total(near)
    parts = [hop(w, ("l", "c"), 4, k) for k in range(4)]
    outgoing = call(
        route_rims_kernel, ((8, 128, 128), BF), (codes, rims), 1, [pltpu.VMEM((1024, 128), F32)]
    )
    ret = octet(outgoing)
    gin, lev = call(
        final_kernel,
        [((2, 32, 4096), BF), ((2, 64, 1024), BF)],
        (glue, ret, keep, rback, perm, edge, rev),
        1,
        [pltpu.VMEM((64, 4096), BF), pltpu.VMEM((512, 512), BF)],
    )
    gc, gl = call(
        unpack_kernel,
        [((9, 32, 64), F32), ((32, 2, 2, 128), F32)],
        tuple(parts),
        0,
        [pltpu.VMEM((288, 128), F32)],
    )
    grad_conv = jnp.transpose(gc.reshape(3, 3, 32, 64), (3, 2, 0, 1))
    grad_level = jnp.transpose(gl, (3, 0, 1, 2))
    return lev, gin, grad_conv, grad_level


def solution(mesh):
    fine = Mesh(mesh.devices.reshape(4, 4, 2, 2, 2), ("z", "x", "l", "c", "h"))
    tile = ("z", "x", "l", "c")
    return jax.shard_map(
        level_step,
        mesh=fine,
        in_specs=(
            P(tile, "h", None),
            P(tile, None, None),
            P(),
            P(),
            P(tile, "h", None),
        ),
        out_specs=(
            P(tile, "h", None),
            P(tile, "h", None),
            P(None, "h", None, None),
            P(None, "h", None, None),
        ),
        check_vma=False,
    )
```
